32 devices in a mesh: mem: 2 (over y), gy: 4 (over z), gx: 4 (over x, core).
Axes of the slice: x: 2, y: 2, z: 4, core: 2. Of those that a mesh axis runs over, the one named last changes fastest.
Arguments:
- perturbations: bfloat16 [4, 5, 16, 32, 512], P('mem', None, None, 'gy', 'gx'), may hold values from -6 to 6
- control: float32 [4, 16, 32, 512], P('mem', None, 'gy', 'gx'), may hold values from -6 to 6
- background: float32 [5, 16, 32, 512], P(None, 'mem', 'gy', 'gx'), may hold values from -6 to 6
- obs_cell: int32 [128, 512], P('gy', 'gx'), may hold values from 0 to 81919
- huber_flag: int32 [128, 512], P('gy', 'gx'), may hold values 0 or 1
- innovation: float32 [128, 512], P('gy', 'gx'), may hold values from -6 to 6
- precision: float32 [128, 512], P('gy', 'gx'), may hold values from 10 to 100
Outputs:
- analysis: float32 [5, 16, 32, 512], P(None, 'mem', 'gy', 'gx')
- control_out: float32 [4, 16, 32, 512], P('mem', None, 'gy', 'gx')
The draws below stay inside these ranges and needn't reach their ends.
Inputs may be any that keep to these rules, and one draw needn't show every extreme that they name: `obs_cell`: a cell of its tile, ordered by variable, then level, then row, then column.
All inputs are finite; a program needn't handle non-finite values. No bound on the sum of `huber_flag` on one device may be relied on, other than what follows from the above.
Results may differ from the reference program's by a relative error of at most 0.0003.
Values sent between devices are 32-bit elements; how exact they have to be, the bound alone decides.
No kernel may reach another device: no remote copies, remote signals or barrier semaphores. Data moves between devices by JAX's collectives and lax.ppermute only.
A program may use at most 64 MiB of HBM per device.

```python
import math
import jax
import jax.numpy as jnp
from jax import lax

VARS = 5
NZ = 16
TY = 8
TX = 128
OBS_R = 32
OBS_C = 128
ITERS = 2
MEMBERS = 4
NY = 32
NX = 512
NOBSY = 128
NOBSX = 512


def place_ends(drawn, stream_key, smallest, largest):
    shape = drawn.shape
    spot = [jax.random.randint(jax.random.fold_in(stream_key, axis), (), 0, shape[axis]) for axis in range(len(shape))]
    drawn = drawn.at[tuple(spot)].set(smallest)
    longest = shape.index(max(shape))
    spot[longest] = (spot[longest] + 1) % shape[longest]
    return drawn.at[tuple(spot)].set(largest)


def with_spikes(result, own_key, source, target, blocks, factor):
    owner, partner = [(jnp.arange(result.shape[axis_at]) // (result.shape[axis_at] // blocks)).reshape([-1 if axis == axis_at else 1 for axis in range(result.ndim)]) for axis_at in (source, target)]
    chosen = jax.random.permutation(own_key, blocks)[partner]
    strong = (owner == chosen) | (owner == (partner + blocks // 2) % blocks)
    return jnp.where(strong, factor * result, result)


def shard_levels(stream_key, shape, shards, low, high):
    factor_of, own = 1.0, jax.random.fold_in(stream_key, 6)
    for dim, parts in shards:
        heights = jnp.exp(jax.random.uniform(jax.random.fold_in(own, dim), (parts,), jnp.float32, low / len(shards), high / len(shards)))
        factor_of = factor_of * jnp.repeat(heights, shape[dim] // parts).reshape([-1 if axis == dim else 1 for axis in range(len(shape))])
    return factor_of


def bell_draw(own_key, dims, scale, most, cuts=(), held_as=jnp.bfloat16):
    drawn = jax.random.normal(own_key, dims, jnp.float32) * scale
    if len(cuts) > 0:
        drawn = shard_levels(own_key, dims, cuts, -0.22, 0.18) * drawn
    return jnp.clip(drawn, min=-most, max=most).astype(held_as)


def bell_draw_with(stream_key, shape, deviation, reach, split, heavy, dtype=jnp.bfloat16):
    drawn = deviation * jax.random.normal(stream_key, shape, jnp.float32)
    if split:
        drawn = drawn * shard_levels(stream_key, shape, split, -0.22, 0.18)
    return jnp.clip(with_spikes(drawn, jax.random.fold_in(stream_key, 3), *heavy), -reach, reach).astype(dtype)


def setup_inputs(seed: int = 0) -> dict:
    splits = jax.random.split(jax.random.key(seed), 8)
    return {
        "perturbations": bell_draw_with(splits[0], (MEMBERS, VARS, NZ, NY, NX), 1.0, 6.0, ((0, 2), (3, 4), (4, 4)), (0, 2, 2, 2.0)),
        "control": bell_draw(splits[1], (MEMBERS, NZ, NY, NX), 1.0, 6.0, ((0, 2), (2, 4), (3, 4)), jnp.float32),
        "background": bell_draw(splits[2], (VARS, NZ, NY, NX), 1.0, 6.0, ((1, 2), (2, 4), (3, 4)), jnp.float32),
        "obs_cell": place_ends(jax.random.randint(splits[3], (NOBSY, NOBSX), 0, VARS * NZ * TY * TX), jax.random.fold_in(splits[3], 1), 0, (VARS * NZ * TY * TX) - 1).astype(jnp.int32),
        "huber_flag": place_ends((jax.random.randint(splits[4], (NOBSY, NOBSX), 0, 3) < 1).astype(jnp.int32), jax.random.fold_in(splits[4], 1), 0, 1),
        "innovation": bell_draw(splits[5], (NOBSY, NOBSX), 1.0, 6.0, ((0, 4), (1, 4)), jnp.float32),
        "precision": jnp.clip(jnp.exp(math.log(100.0) - 2.3025851 * jax.random.uniform(splits[6], (NOBSY, NOBSX), jnp.float32) ** shard_levels(splits[6], (NOBSY, NOBSX), ((0, 4), (1, 4)), -0.2, 0.2)), 10.0, 100.0),
    }


huber_width = 1.0

def filter_taps():
    offsets = jnp.arange(-4, 5).astype(jnp.float32)
    raw = jnp.exp(-offsets * offsets / 8.0)
    return raw / jnp.sum(raw)

def smooth(field):
    weights = filter_taps()
    rows, cols = (field.shape[-2], field.shape[-1])
    widths = [(0, 0)] * (field.ndim - 2) + [(4, 4), (4, 4)]
    padded = jnp.pad(field, widths)
    along = sum((weights[offset] * padded[..., :, offset:offset + cols] for offset in range(9)))
    return sum((weights[offset] * along[..., offset:offset + rows, :] for offset in range(9)))

def member_sum(perturbations, alpha):

    def add_one(total, member_pair):
        member_pert, member_field = member_pair
        return (total + member_pert.astype(jnp.float32) * member_field[None], None)
    start = jnp.zeros(perturbations.shape[1:], jnp.float32)
    total, unused = lax.scan(add_one, start, (perturbations, alpha))
    return total

def project(perturbations, adjoint):
    return lax.map(lambda member_pert: lax.optimization_barrier(jnp.sum(member_pert.astype(jnp.float32) * adjoint, axis=0)), perturbations)

def reference(perturbations, control, background, obs_cell, huber_flag, innovation, precision):
    cells = TY * TX
    var_of = obs_cell // (NZ * cells)
    rest = obs_cell % (NZ * cells)
    level = rest // cells
    spot = rest % cells
    tile_row = (jnp.arange(obs_cell.shape[0]).astype(jnp.int32) // OBS_R)[:, None]
    tile_col = (jnp.arange(obs_cell.shape[1]).astype(jnp.int32) // OBS_C)[None, :]
    grid_row = (tile_row * TY + spot // TX).astype(jnp.int32)
    grid_col = (tile_col * TX + spot % TX).astype(jnp.int32)
    state = control
    increment = member_sum(perturbations, smooth(state))
    for iteration in range(ITERS):
        misfit = increment[var_of, level, grid_row, grid_col] - innovation
        scaled = misfit / huber_width
        weight = jnp.where(huber_flag == 1, 1.0 / jnp.sqrt(1.0 + scaled * scaled), 1.0)
        adjoint = jnp.zeros_like(increment).at[var_of, level, grid_row, grid_col].add(precision * weight * misfit)
        grad = state + smooth(project(perturbations, adjoint))
        delta = member_sum(perturbations, smooth(grad))
        grad_norm = jnp.sum(grad * grad)
        seen_step = delta[var_of, level, grid_row, grid_col]
        curv = jnp.sum(precision * weight * seen_step * seen_step)
        step = grad_norm / (grad_norm + curv)
        state = state - step * grad
        increment = increment - step * delta
    return (background + increment, state)
```

```python
import functools
import math

import jax
import jax.numpy as jnp
from jax import lax
from jax.experimental import pallas as pl
from jax.experimental.pallas import tpu as pltpu
from jax.sharding import PartitionSpec as P

ITERS = 2
RADIUS = 4
RAW = [math.exp(-o * o / 8.0) for o in range(-RADIUS, RADIUS + 1)]
TAPS = [r / sum(RAW) for r in RAW]
HALO = 2 * RADIUS
F32 = jnp.float32
BF16 = jnp.bfloat16
EXACT = lax.Precision.HIGHEST
CHUNK = 4


def iota(shape, dim):
    return lax.broadcasted_iota(jnp.int32, shape, dim)


def over(k, n):
    return lax.shift_right_logical(k, n.bit_length() - 1) if n & (n - 1) == 0 else k // n


def rem(k, n):
    return k & (n - 1) if n & (n - 1) == 0 else k % n


def tap(d):
    d = jnp.abs(d)
    value = jnp.zeros(d.shape, F32)
    for o in range(RADIUS + 1):
        value = jnp.where(d == o, TAPS[RADIUS + o], value)
    return value


def exact_dot(a, b):
    return jnp.dot(a, b, precision=EXACT, preferred_element_type=F32)


def halves(f32):
    high = f32.astype(BF16)
    low = (f32 - high.astype(F32)).astype(BF16)
    return high, low


def split_x(field):
    half = field.shape[0] // 2
    return jnp.concatenate([field[:half], field[half:]], axis=1)


def join_x(field):
    half = field.shape[1] // 2
    return jnp.concatenate([field[:, :half], field[:, half:]], axis=0)


def onehot_rows(index, rows):
    wide = jnp.broadcast_to(index, (rows, index.shape[1]))
    return jnp.where(iota(wide.shape, 0) == wide, 1.0, 0.0).astype(BF16)


def cell_row(cell, zy, tx):
    return over(rem(cell, tx), tx // 2) * zy + rem(over(cell, tx), zy)


def cell_low(cell, tx):
    return rem(cell, tx // 2)


def chunk_of(ref, j):
    return jnp.concatenate([ref[j + i : j + i + 1, :] for i in range(CHUNK)], axis=1)


def store_chunk(ref, j, row):
    wide = row.shape[1] // CHUNK
    for i in range(CHUNK):
        ref[j + i : j + i + 1, :] = row[:, i * wide : (i + 1) * wide]


def y_geometry(k, zy, ty, gy, ngy):
    tile, at = over(k, zy), rem(k, zy)
    side = jnp.where(rem(gy, 2) == 0, 1, -1)
    moved = gy + jnp.where(tile == 0, 0, jnp.where(tile == 1, side, -side))
    return over(at, ty), moved * ty + rem(at, ty), (moved >= 0) & (moved < ngy)


def prep_kernel(pert, cell, flag, innov, prec, info, table):
    members, variables, zy, tx = pert.shape
    half = tx // 2
    for m in range(members):
        for v in range(variables):
            block = split_x(pert[m, v].astype(F32).T)
            at = (m * variables + v) * half
            table[at : at + half, :] = block.astype(BF16)
    for j in range(0, cell.shape[0], CHUNK):
        k = chunk_of(cell, j)
        hot = onehot_rows(cell_row(k, zy, tx), 2 * zy)
        found = jnp.dot(table[...], hot, preferred_element_type=F32)
        want = over(k, tx * zy) * half + cell_low(k, tx)
        rows = variables * half
        mask = iota((rows, k.shape[1]), 0) == jnp.broadcast_to(want, (rows, k.shape[1]))
        for m in range(members):
            mine = jnp.where(mask, found[m * rows : (m + 1) * rows], 0.0)
            store_chunk(info.at[3 + m], j, jnp.sum(mine, axis=0, keepdims=True))
    info[0] = cell[...].astype(F32)
    info[1] = jnp.where(flag[...] == 1, -prec[...], prec[...])
    info[2] = innov[...]


def matrices_kernel(ty, pos, ky, kx):
    wide, zy = ky.shape[0], ky.shape[1] // 2
    tx = kx.shape[1]
    gy, ngy, gx, ngx = pos[0], pos[1], pos[2], pos[3]

    def along_y(shape):
        zs, ys, oks = y_geometry(iota(shape, 0), zy, ty, gy, ngy)
        zt, yt, okt = y_geometry(iota(shape, 1), zy, ty, gy, ngy)
        return jnp.where((zs == zt) & oks & okt, tap(ys - yt), 0.0)

    once = along_y((wide, zy))
    ky[:, :zy] = once
    ky[:, zy:] = exact_dot(along_y((wide, wide)), once)

    def x_of(k):
        at = jnp.where(k < tx, k, jnp.where(k < tx + HALO, k - tx - HALO, k - HALO))
        full = gx * tx + at
        return at, (full >= 0) & (full < ngx * tx)

    def along_x(shape):
        xt, okt = x_of(iota(shape, 0))
        xs, oks = x_of(iota(shape, 1))
        return jnp.where(oks & okt, tap(xs - xt), 0.0)

    long = tx + 2 * HALO
    kx[0] = along_x((tx, long))
    kx[1] = exact_dot(along_x((tx, long)), along_x((long, long)))


def start_kernel(own, a, b, ky, y1, right, left):
    members, zy, tx = own.shape
    for m in range(members):
        wide = jnp.concatenate([own[m].T, a[m].T, b[m].T], axis=1)
        out = exact_dot(wide, ky[:, :zy])
        y1[m] = out
        right[m] = out[tx - HALO :]
        left[m] = out[:HALO]


def x_smooth(matrix, fields, lefts, rights):
    wide = [jnp.concatenate([f, l, r], axis=0) for f, l, r in zip(fields, lefts, rights)]
    out = exact_dot(matrix, jnp.concatenate(wide, axis=1))
    zy = fields[0].shape[1]
    return [out[:, i * zy : (i + 1) * zy] for i in range(len(fields))]


def gather_at(fields, info, seen, tx, zy):
    members, half = len(fields), tx // 2
    parts = [halves(split_x(f)) for f in fields]
    stacked = jnp.concatenate([p[0] for p in parts] + [p[1] for p in parts], axis=0)
    rows = members * half
    for j in range(0, info.shape[1], CHUNK):
        k = chunk_of(info.at[0], j).astype(jnp.int32)
        hot = onehot_rows(cell_row(k, zy, tx), 2 * zy)
        found = jnp.dot(stacked, hot, preferred_element_type=F32)
        low = jnp.broadcast_to(cell_low(k, tx), (half, k.shape[1]))
        mask = iota(low.shape, 0) == low
        total = None
        for m in range(members):
            both = found[m * half : (m + 1) * half] + found[rows + m * half : rows + (m + 1) * half]
            term = jnp.where(mask, both, 0.0) * jnp.broadcast_to(chunk_of(info.at[3 + m], j), both.shape)
            total = term if total is None else total + term
        store_chunk(seen, j, jnp.sum(total, axis=0, keepdims=True))


def first_seen_kernel(y1, from_left, from_right, v, kx, info, smoothed, control, seen):
    members, tx, zy = y1.shape
    outs = x_smooth(kx[0], [y1[m] for m in range(members)], [from_left[m] for m in range(members)], [from_right[m] for m in range(members)])
    for m in range(members):
        smoothed[m] = outs[m]
        control[m] = v[m].T
    gather_at(outs, info, seen, tx, zy)


def step_rows(sums):
    total = jnp.sum(sums, axis=0, keepdims=True)
    lane = iota(total.shape, 1)
    g = jnp.sum(jnp.where(lane == 0, total, 0.0), axis=1, keepdims=True)
    c = jnp.sum(jnp.where(lane == 1, total, 0.0), axis=1, keepdims=True)
    return g / (g + c)


def scatter_kernel(has_step, tx, zy, *refs):
    infos, incs = refs[0:3], refs[3:6]
    refs = refs[6:]
    if has_step:
        steps, sums = refs[0:3], refs[3]
        refs = refs[4:]
        step = step_rows(sums[...])
    ky, y1, y2, right, left, weights, inc_out, vals = refs
    members = infos[0].shape[0] - 3
    half = tx // 2
    tiles = []
    for t in range(3):
        info = infos[t]
        inc = incs[t][...]
        if has_step:
            inc = inc - step * steps[t][...]
        misfit = inc - info[2]
        prec = info[1]
        weight = jnp.where(prec < 0, 1.0 / jnp.sqrt(1.0 + misfit * misfit), 1.0)
        pw = jnp.abs(prec) * weight
        q = pw * misfit
        if t == 0:
            weights[...] = pw
            inc_out[...] = inc
        for m in range(members):
            val = info[3 + m] * q
            high = val.astype(BF16).astype(F32)
            vals[2 * m] = high
            vals[2 * m + 1] = val - high
        acc = None
        for j in range(0, info.shape[1], CHUNK):
            k = chunk_of(info.at[0], j).astype(jnp.int32)
            hot = onehot_rows(cell_row(k, zy, tx), 2 * zy)
            low = jnp.broadcast_to(cell_low(k, tx), (half, k.shape[1]))
            mask = iota(low.shape, 0) == low
            rows = []
            for i in range(2 * members):
                row = jnp.broadcast_to(chunk_of(vals.at[i], j), low.shape)
                rows.append(jnp.where(mask, row, 0.0).astype(BF16))
            part = lax.dot_general(jnp.concatenate(rows, axis=0), hot, (((1,), (1,)), ((), ())), preferred_element_type=F32)
            acc = part if acc is None else acc + part
        fields = []
        for m in range(members):
            at = 2 * m * half
            fields.append(join_x(acc[at : at + half] + acc[at + half : at + 2 * half]))
        tiles.append(jnp.concatenate(fields, axis=0))
    out = exact_dot(jnp.concatenate(tiles, axis=1), ky[...])
    for m in range(members):
        for i, y in enumerate((y1, y2)):
            field = out[m * tx : (m + 1) * tx, i * zy : (i + 1) * zy]
            y[m] = field
            right[i, m] = field[tx - HALO :]
            left[i, m] = field[:HALO]


def gather_kernel(has_step, *refs):
    y1, y2, from_left, from_right, kx, info, control, smoothed = refs[:8]
    refs = refs[8:]
    members, tx, zy = y1.shape
    if has_step:
        old_grad, old_smooth, sums, new_control, new_smoothed = refs[:5]
        refs = refs[5:]
        step = step_rows(sums[...])
    grad_out, smooth_out, seen, gnorm = refs
    each = range(members)
    once = x_smooth(kx[0], [y1[m] for m in each], [from_left[0, m] for m in each], [from_right[0, m] for m in each])
    twice = x_smooth(kx[1], [y2[m] for m in each], [from_left[1, m] for m in each], [from_right[1, m] for m in each])
    squares = None
    outs = []
    for m in each:
        v, s = control[m], smoothed[m]
        if has_step:
            v = v - step * old_grad[m]
            s = s - step * old_smooth[m]
            new_control[m] = v
            new_smoothed[m] = s
        grad = v + once[m]
        smooth_grad = s + twice[m]
        grad_out[m] = grad
        smooth_out[m] = smooth_grad
        outs.append(smooth_grad)
        part = jnp.sum(grad * grad, axis=0, keepdims=True)
        squares = part if squares is None else squares + part
    gnorm[...] = squares
    gather_at(outs, info, seen, tx, zy)


def curv_kernel(pos, mine, other, weights, gnorm, seen, sums):
    total = mine[...] + other[...]
    seen[...] = total
    counted = jnp.where(pos[4] == 0, 1.0, 0.0)
    c = jnp.sum(jnp.sum(weights[...] * total * total, axis=0, keepdims=True), axis=1, keepdims=True) * counted
    g = jnp.sum(gnorm[...], axis=1, keepdims=True)
    lane = iota(sums.shape, 1)
    sums[...] = jnp.where(lane == 0, g, jnp.where(lane == 1, c, 0.0))


def final_kernel(pos, sums, control, smoothed, grad, smooth_grad, pert, control_out, keep, send):
    members, tx, zy = control.shape
    variables = pert.shape[1]
    step = step_rows(sums[...])
    fields = []
    for m in range(members):
        control_out[m] = (control[m] - step * grad[m]).T
        fields.append((smoothed[m] - step * smooth_grad[m]).T)
    rows = keep.shape[1]
    for v in range(variables):
        inc = None
        for m in range(members):
            term = pert[m, v].astype(F32) * fields[m]
            inc = term if inc is None else inc + term
        low, high = inc[:rows], inc[rows:]
        first = pos[4] == 0
        keep[v] = jnp.where(first, low, high)
        send[v] = jnp.where(first, high, low)


VMEM = pl.BlockSpec(memory_space=pltpu.VMEM)
SMEM = pl.BlockSpec(memory_space=pltpu.SMEM)


def call(kernel, ins, outs, scratch=(), smem=0, us=3.0, name=None):
    shapes = [jax.ShapeDtypeStruct(s, F32) for s in outs]
    return pl.pallas_call(
        kernel,
        out_shape=shapes,
        in_specs=[SMEM] * smem + [VMEM] * (len(ins) - smem),
        out_specs=[VMEM] * len(outs),
        scratch_shapes=list(scratch),
        cost_estimate=pl.CostEstimate(flops=int(us * 1e9), bytes_accessed=1 << 20, transcendentals=0),
        name=name,
    )(*ins)


def pairs_a(n):
    return [(i, i ^ 1 if i ^ 1 < n else i) for i in range(n)]


def pairs_b(n):
    to = [((i + 1) ^ 1) - 1 for i in range(n)]
    return [(i, t if 0 <= t < n else i) for i, t in enumerate(to)]


def both_y(value):
    n = lax.axis_size("gy")
    return lax.ppermute(value, "gy", pairs_a(n)), lax.ppermute(value, "gy", pairs_b(n))


def both_x(right, left):
    n = lax.axis_size("gx")
    up = [(i, (i + 1) % n) for i in range(n)]
    down = [(j, i) for i, j in up]
    return lax.ppermute(right, "gx", up), lax.ppermute(left, "gx", down)


def other_members(value):
    n = lax.axis_size("mem")
    if n == 2:
        return lax.ppermute(value, "mem", [(0, 1), (1, 0)])
    return lax.psum(value, "mem") - value


def per_device(perturbations, control, background, obs_cell, huber_flag, innovation, precision):
    members, variables, nz, ty, tx = perturbations.shape
    zy = nz * ty
    obs = obs_cell.shape
    axes = ("mem", "gy", "gx")
    pos = jnp.stack([lax.axis_index("gy"), lax.axis_size("gy"), lax.axis_index("gx"), lax.axis_size("gx"), lax.axis_index("mem")]).astype(jnp.int32)
    n_all = math.prod(lax.axis_size(a) for a in axes)
    pert = perturbations.reshape(members, variables, zy, tx)
    field = (members, tx, zy)
    strip = (members, HALO, zy)

    own = control.reshape(members, zy, tx)
    above, below = both_y(own)
    (info,) = call(
        prep_kernel,
        [pert, obs_cell, huber_flag, innovation, precision],
        [(3 + members,) + obs],
        [pltpu.VMEM((members * variables * tx // 2, 2 * zy), BF16)],
        us=6.0,
        name="prep",
    )
    ky, kx = call(functools.partial(matrices_kernel, ty), [pos], [(3 * zy, 2 * zy), (2, tx, tx + 2 * HALO)], smem=1, us=3.0, name="matrices")
    y1, right, left = call(start_kernel, [own, above, below, ky], [field, strip, strip], us=1.5, name="start")
    from_left, from_right = both_x(right, left)
    smoothed, state, seen_part = call(first_seen_kernel, [y1, from_left, from_right, own, kx, info], [field, field, obs], us=3.0, name="first_seen")
    inc = seen_part + other_members(seen_part)
    packed = jnp.concatenate([info, inc[None]], axis=0)
    packs = (packed,) + both_y(packed)
    infos = [p[:-1] for p in packs]
    incs = [p[-1] for p in packs]
    steps, sums, grad, smooth_grad = None, None, None, None
    double = (2,) + strip
    for iteration in range(ITERS):
        later = iteration > 0
        ins = infos + incs + (steps + [sums] if later else []) + [ky]
        y1, y2, right, left, weights, own_inc = call(
            functools.partial(scatter_kernel, later, tx, zy),
            ins,
            [field, field, double, double, obs, obs],
            [pltpu.VMEM((2 * members,) + obs, F32)],
            us=6.0,
            name="scatter",
        )
        from_left, from_right = both_x(right, left)
        ins = [y1, y2, from_left, from_right, kx, info, state, smoothed]
        outs = [field, field, obs, (1, zy)]
        if later:
            ins += [grad, smooth_grad, sums]
            outs = [field, field] + outs
        result = call(functools.partial(gather_kernel, later), ins, outs, us=4.0, name="gather")
        if later:
            state, smoothed = result[:2]
        grad, smooth_grad, seen_part, gnorm = result[-4:]
        seen_step, to_all = call(curv_kernel, [pos, seen_part, other_members(seen_part), weights, gnorm], [obs, (n_all, 128)], smem=1, us=1.0, name="curv")
        if iteration + 1 < ITERS:
            steps = [seen_step, *both_y(seen_step)]
        sums = lax.all_to_all(to_all, axes, 0, 0, tiled=True)
    n_mem = lax.axis_size("mem")
    part = (variables, zy // 2, tx)
    if n_mem == 2:
        control_out, keep, send = call(final_kernel, [pos, sums, state, smoothed, grad, smooth_grad, pert], [(members, zy, tx), part, part], smem=1, us=3.0, name="final")
        mine = keep + lax.ppermute(send, "mem", [(0, 1), (1, 0)])
    else:
        control_out, low, high = call(final_kernel, [pos * 0, sums, state, smoothed, grad, smooth_grad, pert], [(members, zy, tx), part, part], smem=1, us=3.0, name="final")
        mine = lax.psum_scatter(jnp.concatenate([low, high], axis=1), "mem", scatter_dimension=1, tiled=True)
    return background + mine.reshape(background.shape), control_out.reshape(control.shape)


def solution(mesh):
    in_specs = (
        P("mem", None, None, "gy", "gx"),
        P("mem", None, "gy", "gx"),
        P(None, "mem", "gy", "gx"),
        P("gy", "gx"),
        P("gy", "gx"),
        P("gy", "gx"),
        P("gy", "gx"),
    )
    out_specs = (P(None, "mem", "gy", "gx"), P("mem", None, "gy", "gx"))
    return jax.shard_map(per_device, mesh=mesh, in_specs=in_specs, out_specs=out_specs, check_vma=False)
```

```python
import functools
import math

import jax
import jax.numpy as jnp
from jax import lax
from jax.experimental import pallas as pl
from jax.experimental.pallas import tpu as pltpu
from jax.sharding import PartitionSpec as P

ITERS = 2
RADIUS = 4
RAW = [math.exp(-o * o / 8.0) for o in range(-RADIUS, RADIUS + 1)]
TAPS = [r / sum(RAW) for r in RAW]
HALO = 2 * RADIUS
F32 = jnp.float32
BF16 = jnp.bfloat16
EXACT = lax.Precision.HIGHEST
CHUNK = 4


def iota(shape, dim):
    return lax.broadcasted_iota(jnp.int32, shape, dim)


def over(k, n):
    return lax.shift_right_logical(k, n.bit_length() - 1) if n & (n - 1) == 0 else k // n


def rem(k, n):
    return k & (n - 1) if n & (n - 1) == 0 else k % n


def tap(d):
    d = jnp.abs(d)
    value = jnp.zeros(d.shape, F32)
    for o in range(RADIUS + 1):
        value = jnp.where(d == o, TAPS[RADIUS + o], value)
    return value


def exact_dot(a, b):
    return jnp.dot(a, b, precision=EXACT, preferred_element_type=F32)


def halves(f32):
    high = f32.astype(BF16)
    low = (f32 - high.astype(F32)).astype(BF16)
    return high, low


def split_x(field):
    half = field.shape[0] // 2
    return jnp.concatenate([field[:half], field[half:]], axis=1)


def join_x(field):
    half = field.shape[1] // 2
    return jnp.concatenate([field[:, :half], field[:, half:]], axis=0)


def onehot_rows(index, rows):
    wide = jnp.broadcast_to(index, (rows, index.shape[1]))
    return jnp.where(iota(wide.shape, 0) == wide, 1.0, 0.0).astype(BF16)


def cell_row(cell, zy, tx):
    return over(rem(cell, tx), tx // 2) * zy + rem(over(cell, tx), zy)


def cell_low(cell, tx):
    return rem(cell, tx // 2)


def chunk_of(ref, j):
    return jnp.concatenate([ref[j + i : j + i + 1, :] for i in range(CHUNK)], axis=1)


def store_chunk(ref, j, row):
    wide = row.shape[1] // CHUNK
    for i in range(CHUNK):
        ref[j + i : j + i + 1, :] = row[:, i * wide : (i + 1) * wide]


def y_geometry(k, zy, ty, gy, ngy):
    tile, at = over(k, zy), rem(k, zy)
    side = jnp.where(rem(gy, 2) == 0, 1, -1)
    moved = gy + jnp.where(tile == 0, 0, jnp.where(tile == 1, side, -side))
    return over(at, ty), moved * ty + rem(at, ty), (moved >= 0) & (moved < ngy)


def prep_kernel(pert, cell, flag, innov, prec, info, table):
    members, variables, zy, tx = pert.shape
    half = tx // 2
    for m in range(members):
        for v in range(variables):
            block = split_x(pert[m, v].astype(F32).T)
            at = (m * variables + v) * half
            table[at : at + half, :] = block.astype(BF16)
    for j in range(0, cell.shape[0], CHUNK):
        k = chunk_of(cell, j)
        hot = onehot_rows(cell_row(k, zy, tx), 2 * zy)
        found = jnp.dot(table[...], hot, preferred_element_type=F32)
        want = over(k, tx * zy) * half + cell_low(k, tx)
        rows = variables * half
        mask = iota((rows, k.shape[1]), 0) == jnp.broadcast_to(want, (rows, k.shape[1]))
        for m in range(members):
            mine = jnp.where(mask, found[m * rows : (m + 1) * rows], 0.0)
            store_chunk(info.at[3 + m], j, jnp.sum(mine, axis=0, keepdims=True))
    info[0] = cell[...].astype(F32)
    info[1] = jnp.where(flag[...] == 1, -prec[...], prec[...])
    info[2] = innov[...]


def matrices_kernel(ty, pos, ky, kx):
    wide, zy = ky.shape[0], ky.shape[1] // 2
    tx = kx.shape[1]
    gy, ngy, gx, ngx = pos[0], pos[1], pos[2], pos[3]

    def along_y(shape):
        zs, ys, oks = y_geometry(iota(shape, 0), zy, ty, gy, ngy)
        zt, yt, okt = y_geometry(iota(shape, 1), zy, ty, gy, ngy)
        return jnp.where((zs == zt) & oks & okt, tap(ys - yt), 0.0)

    once = along_y((wide, zy))
    ky[:, :zy] = once
    ky[:, zy:] = exact_dot(along_y((wide, wide)), once)

    def x_of(k):
        at = jnp.where(k < tx, k, jnp.where(k < tx + HALO, k - tx - HALO, k - HALO))
        full = gx * tx + at
        return at, (full >= 0) & (full < ngx * tx)

    def along_x(shape):
        xt, okt = x_of(iota(shape, 0))
        xs, oks = x_of(iota(shape, 1))
        return jnp.where(oks & okt, tap(xs - xt), 0.0)

    long = tx + 2 * HALO
    kx[0] = along_x((tx, long))
    kx[1] = exact_dot(along_x((tx, long)), along_x((long, long)))


def start_kernel(own, a, b, ky, y1, right, left):
    members, zy, tx = own.shape
    for m in range(members):
        wide = jnp.concatenate([own[m].T, a[m].T, b[m].T], axis=1)
        out = exact_dot(wide, ky[:, :zy])
        y1[m] = out
        right[m] = out[tx - HALO :]
        left[m] = out[:HALO]


def x_smooth(matrix, fields, lefts, rights):
    wide = [jnp.concatenate([f, l, r], axis=0) for f, l, r in zip(fields, lefts, rights)]
    out = exact_dot(matrix, jnp.concatenate(wide, axis=1))
    zy = fields[0].shape[1]
    return [out[:, i * zy : (i + 1) * zy] for i in range(len(fields))]


def gather_at(fields, info, seen, tx, zy):
    members, half = len(fields), tx // 2
    parts = [halves(split_x(f)) for f in fields]
    stacked = jnp.concatenate([p[0] for p in parts] + [p[1] for p in parts], axis=0)
    rows = members * half
    for j in range(0, info.shape[1], CHUNK):
        k = chunk_of(info.at[0], j).astype(jnp.int32)
        hot = onehot_rows(cell_row(k, zy, tx), 2 * zy)
        found = jnp.dot(stacked, hot, preferred_element_type=F32)
        low = jnp.broadcast_to(cell_low(k, tx), (half, k.shape[1]))
        mask = iota(low.shape, 0) == low
        total = None
        for m in range(members):
            both = found[m * half : (m + 1) * half] + found[rows + m * half : rows + (m + 1) * half]
            term = jnp.where(mask, both, 0.0) * jnp.broadcast_to(chunk_of(info.at[3 + m], j), both.shape)
            total = term if total is None else total + term
        store_chunk(seen, j, jnp.sum(total, axis=0, keepdims=True))


def first_seen_kernel(y1, from_left, from_right, v, kx, info, smoothed, control, seen):
    members, tx, zy = y1.shape
    outs = x_smooth(kx[0], [y1[m] for m in range(members)], [from_left[m] for m in range(members)], [from_right[m] for m in range(members)])
    for m in range(members):
        smoothed[m] = outs[m]
        control[m] = v[m].T
    gather_at(outs, info, seen, tx, zy)


def step_rows(sums):
    total = jnp.sum(sums, axis=0, keepdims=True)
    lane = iota(total.shape, 1)
    g = jnp.sum(jnp.where(lane == 0, total, 0.0), axis=1, keepdims=True)
    c = jnp.sum(jnp.where(lane == 1, total, 0.0), axis=1, keepdims=True)
    return g / (g + c)


def scatter_kernel(has_step, tx, zy, *refs):
    infos, incs = refs[0:3], refs[3:6]
    refs = refs[6:]
    if has_step:
        steps, sums = refs[0:3], refs[3]
        refs = refs[4:]
        step = step_rows(sums[...])
    ky, y1, y2, right, left, weights, inc_out, vals = refs
    members = infos[0].shape[0] - 3
    half = tx // 2
    tiles = []
    for t in range(3):
        info = infos[t]
        inc = incs[t][...]
        if has_step:
            inc = inc - step * steps[t][...]
        misfit = inc - info[2]
        prec = info[1]
        weight = jnp.where(prec < 0, 1.0 / jnp.sqrt(1.0 + misfit * misfit), 1.0)
        pw = jnp.abs(prec) * weight
        q = pw * misfit
        if t == 0:
            weights[...] = pw
            inc_out[...] = inc
        for m in range(members):
            val = info[3 + m] * q
            high = val.astype(BF16).astype(F32)
            vals[2 * m] = high
            vals[2 * m + 1] = val - high
        acc = None
        for j in range(0, info.shape[1], CHUNK):
            k = chunk_of(info.at[0], j).astype(jnp.int32)
            hot = onehot_rows(cell_row(k, zy, tx), 2 * zy)
            low = jnp.broadcast_to(cell_low(k, tx), (half, k.shape[1]))
            mask = iota(low.shape, 0) == low
            rows = []
            for i in range(2 * members):
                row = jnp.broadcast_to(chunk_of(vals.at[i], j), low.shape)
                rows.append(jnp.where(mask, row, 0.0).astype(BF16))
            part = lax.dot_general(jnp.concatenate(rows, axis=0), hot, (((1,), (1,)), ((), ())), preferred_element_type=F32)
            acc = part if acc is None else acc + part
        fields = []
        for m in range(members):
            at = 2 * m * half
            fields.append(join_x(acc[at : at + half] + acc[at + half : at + 2 * half]))
        tiles.append(jnp.concatenate(fields, axis=0))
    out = exact_dot(jnp.concatenate(tiles, axis=1), ky[...])
    for m in range(members):
        for i, y in enumerate((y1, y2)):
            field = out[m * tx : (m + 1) * tx, i * zy : (i + 1) * zy]
            y[m] = field
            right[i, m] = field[tx - HALO :]
            left[i, m] = field[:HALO]


def gather_kernel(has_step, *refs):
    y1, y2, from_left, from_right, kx, info, control, smoothed = refs[:8]
    refs = refs[8:]
    members, tx, zy = y1.shape
    if has_step:
        old_grad, old_smooth, sums, new_control, new_smoothed = refs[:5]
        refs = refs[5:]
        step = step_rows(sums[...])
    grad_out, smooth_out, seen, gnorm = refs
    each = range(members)
    once = x_smooth(kx[0], [y1[m] for m in each], [from_left[0, m] for m in each], [from_right[0, m] for m in each])
    twice = x_smooth(kx[1], [y2[m] for m in each], [from_left[1, m] for m in each], [from_right[1, m] for m in each])
    squares = None
    outs = []
    for m in each:
        v, s = control[m], smoothed[m]
        if has_step:
            v = v - step * old_grad[m]
            s = s - step * old_smooth[m]
            new_control[m] = v
            new_smoothed[m] = s
        grad = v + once[m]
        smooth_grad = s + twice[m]
        grad_out[m] = grad
        smooth_out[m] = smooth_grad
        outs.append(smooth_grad)
        part = jnp.sum(grad * grad, axis=0, keepdims=True)
        squares = part if squares is None else squares + part
    gnorm[...] = squares
    gather_at(outs, info, seen, tx, zy)


def curv_kernel(pos, mine, other, weights, gnorm, seen, sums):
    total = mine[...] + other[...]
    seen[...] = total
    counted = jnp.where(pos[4] == 0, 1.0, 0.0)
    c = jnp.sum(jnp.sum(weights[...] * total * total, axis=0, keepdims=True), axis=1, keepdims=True) * counted
    g = jnp.sum(gnorm[...], axis=1, keepdims=True)
    lane = iota(sums.shape, 1)
    sums[...] = jnp.where(lane == 0, g, jnp.where(lane == 1, c, 0.0))


def final_kernel(pos, sums, control, smoothed, grad, smooth_grad, pert, control_out, keep, send):
    members, tx, zy = control.shape
    variables = pert.shape[1]
    step = step_rows(sums[...])
    fields = []
    for m in range(members):
        control_out[m] = (control[m] - step * grad[m]).T
        fields.append((smoothed[m] - step * smooth_grad[m]).T)
    rows = keep.shape[1]
    for v in range(variables):
        inc = None
        for m in range(members):
            term = pert[m, v].astype(F32) * fields[m]
            inc = term if inc is None else inc + term
        low, high = inc[:rows], inc[rows:]
        first = pos[4] == 0
        keep[v] = jnp.where(first, low, high)
        send[v] = jnp.where(first, high, low)


VMEM = pl.BlockSpec(memory_space=pltpu.VMEM)
SMEM = pl.BlockSpec(memory_space=pltpu.SMEM)


def call(kernel, ins, outs, scratch=(), smem=0, us=3.0, name=None):
    shapes = [jax.ShapeDtypeStruct(s, F32) for s in outs]
    return pl.pallas_call(
        kernel,
        out_shape=shapes,
        in_specs=[SMEM] * smem + [VMEM] * (len(ins) - smem),
        out_specs=[VMEM] * len(outs),
        scratch_shapes=list(scratch),
        compiler_params=pltpu.CompilerParams(vmem_limit_bytes=16 << 20),
        cost_estimate=pl.CostEstimate(flops=int(us * 1e9), bytes_accessed=1 << 20, transcendentals=0),
        name=name,
    )(*ins)


def pairs_a(n):
    return [(i, i ^ 1 if i ^ 1 < n else i) for i in range(n)]


def pairs_b(n):
    to = [((i + 1) ^ 1) - 1 for i in range(n)]
    return [(i, t if 0 <= t < n else i) for i, t in enumerate(to)]


def both_y(value):
    n = lax.axis_size("gy")
    return lax.ppermute(value, "gy", pairs_a(n)), lax.ppermute(value, "gy", pairs_b(n))


def both_x(right, left):
    n = lax.axis_size("gx")
    up = [(i, (i + 1) % n) for i in range(n)]
    down = [(j, i) for i, j in up]
    return lax.ppermute(right, "gx", up), lax.ppermute(left, "gx", down)


def other_members(value):
    n = lax.axis_size("mem")
    if n == 2:
        return lax.ppermute(value, "mem", [(0, 1), (1, 0)])
    return lax.psum(value, "mem") - value


def per_device(perturbations, control, background, obs_cell, huber_flag, innovation, precision):
    members, variables, nz, ty, tx = perturbations.shape
    zy = nz * ty
    obs = obs_cell.shape
    axes = ("mem", "gy", "gx")
    pos = jnp.stack([lax.axis_index("gy"), lax.axis_size("gy"), lax.axis_index("gx"), lax.axis_size("gx"), lax.axis_index("mem")]).astype(jnp.int32)
    n_all = math.prod(lax.axis_size(a) for a in axes)
    pert = perturbations.reshape(members, variables, zy, tx)
    field = (members, tx, zy)
    strip = (members, HALO, zy)

    own = control.reshape(members, zy, tx)
    above, below = both_y(own)
    (info,) = call(
        prep_kernel,
        [pert, obs_cell, huber_flag, innovation, precision],
        [(3 + members,) + obs],
        [pltpu.VMEM((members * variables * tx // 2, 2 * zy), BF16)],
        us=6.0,
        name="prep",
    )
    ky, kx = call(functools.partial(matrices_kernel, ty), [pos], [(3 * zy, 2 * zy), (2, tx, tx + 2 * HALO)], smem=1, us=3.0, name="matrices")
    y1, right, left = call(start_kernel, [own, above, below, ky], [field, strip, strip], us=1.5, name="start")
    from_left, from_right = both_x(right, left)
    smoothed, state, seen_part = call(first_seen_kernel, [y1, from_left, from_right, own, kx, info], [field, field, obs], us=3.0, name="first_seen")
    inc = seen_part + other_members(seen_part)
    packed = jnp.concatenate([info, inc[None]], axis=0)
    packs = (packed,) + both_y(packed)
    infos = [p[:-1] for p in packs]
    incs = [p[-1] for p in packs]
    steps, sums, grad, smooth_grad = None, None, None, None
    double = (2,) + strip
    for iteration in range(ITERS):
        later = iteration > 0
        ins = infos + incs + (steps + [sums] if later else []) + [ky]
        y1, y2, right, left, weights, own_inc = call(
            functools.partial(scatter_kernel, later, tx, zy),
            ins,
            [field, field, double, double, obs, obs],
            [pltpu.VMEM((2 * members,) + obs, F32)],
            us=6.0,
            name="scatter",
        )
        from_left, from_right = both_x(right, left)
        ins = [y1, y2, from_left, from_right, kx, info, state, smoothed]
        outs = [field, field, obs, (1, zy)]
        if later:
            ins += [grad, smooth_grad, sums]
            outs = [field, field] + outs
        result = call(functools.partial(gather_kernel, later), ins, outs, us=4.0, name="gather")
        if later:
            state, smoothed = result[:2]
        grad, smooth_grad, seen_part, gnorm = result[-4:]
        seen_step, to_all = call(curv_kernel, [pos, seen_part, other_members(seen_part), weights, gnorm], [obs, (n_all, 128)], smem=1, us=1.0, name="curv")
        if iteration + 1 < ITERS:
            steps = [seen_step, *both_y(seen_step)]
        sums = lax.all_to_all(to_all, axes, 0, 0, tiled=True)
    n_mem = lax.axis_size("mem")
    part = (variables, zy // 2, tx)
    if n_mem == 2:
        control_out, keep, send = call(final_kernel, [pos, sums, state, smoothed, grad, smooth_grad, pert], [(members, zy, tx), part, part], smem=1, us=3.0, name="final")
        mine = keep + lax.ppermute(send, "mem", [(0, 1), (1, 0)])
    else:
        control_out, low, high = call(final_kernel, [pos * 0, sums, state, smoothed, grad, smooth_grad, pert], [(members, zy, tx), part, part], smem=1, us=3.0, name="final")
        mine = lax.psum_scatter(jnp.concatenate([low, high], axis=1), "mem", scatter_dimension=1, tiled=True)
    return background + mine.reshape(background.shape), control_out.reshape(control.shape)


def solution(mesh):
    in_specs = (
        P("mem", None, None, "gy", "gx"),
        P("mem", None, "gy", "gx"),
        P(None, "mem", "gy", "gx"),
        P("gy", "gx"),
        P("gy", "gx"),
        P("gy", "gx"),
        P("gy", "gx"),
    )
    out_specs = (P(None, "mem", "gy", "gx"), P("mem", None, "gy", "gx"))
    return jax.shard_map(per_device, mesh=mesh, in_specs=in_specs, out_specs=out_specs, check_vma=False)
```

```python
import functools
import math

import jax
import jax.numpy as jnp
from jax import lax
from jax.experimental import pallas as pl
from jax.experimental.pallas import tpu as pltpu
from jax.sharding import PartitionSpec as P


ITERS = 2
RADIUS = 4
RAW = [math.exp(-o * o / 8.0) for o in range(-RADIUS, RADIUS + 1)]
TAPS = [r / sum(RAW) for r in RAW]
HALO = 2 * RADIUS
F32 = jnp.float32
BF16 = jnp.bfloat16
EXACT = lax.Precision.HIGHEST
CHUNK = 4


def iota(shape, dim):
    return lax.broadcasted_iota(jnp.int32, shape, dim)


def over(k, n):
    return lax.shift_right_logical(k, n.bit_length() - 1) if n & (n - 1) == 0 else k // n


def rem(k, n):
    return k & (n - 1) if n & (n - 1) == 0 else k % n


def tap(d):
    d = jnp.abs(d)
    value = jnp.zeros(d.shape, F32)
    for o in range(RADIUS + 1):
        value = jnp.where(d == o, TAPS[RADIUS + o], value)
    return value


def exact_dot(a, b):
    return jnp.dot(a, b, precision=EXACT, preferred_element_type=F32)


def halves(f32):
    high = f32.astype(BF16)
    low = (f32 - high.astype(F32)).astype(BF16)
    return high, low


def at_lane_block(shape, wide, s):
    return over(iota(shape, 1), wide) == s


def moved(piece, source, target, wide):
    if source == target:
        return piece
    return pltpu.roll(piece, (target - source) * wide % piece.shape[1], 1)


def chunks(tx, wide, lanes):
    parts = 2 * lanes // wide
    return parts, tx // parts


def to_table(groups, wide):
    tx, lanes = groups[0].shape
    parts, short = chunks(tx, wide, lanes)
    per = lanes // wide
    tables = []
    for group in groups:
        for m in range(per):
            blocks = []
            for p in range(parts // per):
                block = None
                for s in range(per):
                    at = (p * per + s) * short
                    piece = moved(group[at : at + short], m, s, wide)
                    block = piece if block is None else jnp.where(at_lane_block(piece.shape, wide, s), piece, block)
                blocks.append(block)
            tables.append(jnp.concatenate(blocks, axis=1))
    return tables


def from_table(tables, wide, lanes):
    per = lanes // wide
    parts = tables[0].shape[1] // wide
    groups = []
    for first in range(0, len(tables), per):
        rows = []
        for x in range(parts):
            p, s = x // per, x % per
            block = None
            for m in range(per):
                piece = moved(tables[first + m][:, p * lanes : (p + 1) * lanes], s, m, wide)
                block = piece if block is None else jnp.where(at_lane_block(piece.shape, wide, m), piece, block)
            rows.append(block)
        groups.append(jnp.concatenate(rows, axis=0))
    return groups


def split_x(field):
    half = field.shape[0] // 2
    return jnp.concatenate([field[:half], field[half:]], axis=1)


def onehot_rows(index, rows):
    wide = jnp.broadcast_to(index, (rows, index.shape[1]))
    return jnp.where(iota(wide.shape, 0) == wide, 1.0, 0.0).astype(BF16)


def chunk_of(ref, j):
    return jnp.concatenate([ref[j + i : j + i + 1, :] for i in range(CHUNK)], axis=1)


def store_chunk(ref, j, row):
    wide = row.shape[1] // CHUNK
    for i in range(CHUNK):
        ref[j + i : j + i + 1, :] = row[:, i * wide : (i + 1) * wide]


def pair_side(index):
    return jnp.where(rem(index, 2) == 0, 1, -1)


def y_geometry(k, zy, ty):
    gy, ngy = lax.axis_index("gy"), lax.axis_size("gy")
    tile, at = over(k, zy), rem(k, zy)
    side = pair_side(gy)
    where = gy + jnp.where(tile == 0, 0, jnp.where(tile == 1, side, -side))
    return over(at, ty), where * ty + rem(at, ty), (where >= 0) & (where < ngy)


def matrices(ty, ky, ky_first, kx):
    wide, zy = ky.shape[0], ky.shape[1] // 2
    tx = kx.shape[1]

    def along_y(shape):
        zs, ys, oks = y_geometry(iota(shape, 0), zy, ty)
        zt, yt, okt = y_geometry(iota(shape, 1), zy, ty)
        return jnp.where((zs == zt) & oks & okt, tap(ys - yt), 0.0)

    once = along_y((wide, zy))
    ky[:, :zy] = once
    ky[:, zy:] = exact_dot(along_y((wide, wide)), once)

    shape = ky_first.shape
    k = iota(shape, 0)
    gy, ngy = lax.axis_index("gy"), lax.axis_size("gy")
    tile = jnp.where(k < zy, 0, jnp.where(k < zy + zy * RADIUS // ty, 1, 2))
    at = k - jnp.where(tile == 0, 0, jnp.where(tile == 1, zy, zy + zy * RADIUS // ty))
    side = jnp.where(tile == 1, pair_side(gy), -pair_side(gy))
    strip_row = (gy + side) * ty + rem(at, RADIUS) + jnp.where(side == 1, 0, ty - RADIUS)
    row = jnp.where(tile == 0, gy * ty + rem(at, ty), strip_row)
    level = jnp.where(tile == 0, over(at, ty), over(at, RADIUS))
    zt, yt, _ = y_geometry(iota(shape, 1), zy, ty)
    ky_first[...] = jnp.where((level == zt) & (row >= 0) & (row < ngy * ty), tap(row - yt), 0.0)
    gx, ngx = lax.axis_index("gx"), lax.axis_size("gx")
    side = pair_side(gx)

    def x_of(k):
        tile, r = jnp.where(k < tx, 0, jnp.where(k < tx + HALO, 1, 2)), rem(k - tx, HALO)
        right = (tile == 1) == (side == 1)
        at = jnp.where(tile == 0, k, jnp.where(right, tx + r, r - HALO))
        full = gx * tx + at
        return at, (full >= 0) & (full < ngx * tx)

    def along_x(shape):
        xt, okt = x_of(iota(shape, 0))
        xs, oks = x_of(iota(shape, 1))
        return jnp.where(oks & okt, tap(xs - xt), 0.0)

    long = tx + 2 * HALO
    kx[0] = along_x((tx, long))
    kx[1] = exact_dot(along_x((tx, long)), along_x((long, long)))


def halves_kernel(control, mine, theirs, sems):
    members, zy, _ = control.shape
    wide = zy // 2
    mem = lax.axis_index("mem")
    copies = []
    for m in range(members):
        for i, (target, part) in enumerate(((theirs, 1 - mem), (mine, mem))):
            source = control.at[m, pl.ds(pl.multiple_of(part * wide, wide), wide), :]
            copies.append(pltpu.make_async_copy(source, target.at[pl.ds(m * wide, wide), :], sems.at[m, i]))
    for copy in copies:
        copy.start()
    for copy in copies:
        copy.wait()


def strips_kernel(ty, *refs):
    *blocks, first, second = refs
    lanes, tx = blocks[0].shape
    next_first = pair_side(lax.axis_index("gy")) == 1
    rows = lanes * RADIUS // ty
    for b, block in enumerate(blocks):
        value = block[...].reshape(lanes // (2 * ty), 2, ty, tx)
        even, odd = value[:, 0], value[:, 1]
        low = iota(even.shape, 1) < RADIUS
        last = jnp.where(low, pltpu.roll(even, RADIUS, 1), odd).reshape(rows, tx)
        initial = jnp.where(low, even, pltpu.roll(odd, RADIUS, 1)).reshape(rows, tx)
        first[b * rows : (b + 1) * rows] = jnp.where(next_first, last, initial)
        second[b * rows : (b + 1) * rows] = jnp.where(next_first, initial, last)


def prep_kernel(ty, wide, pert_in, cell_in, flag_in, innov_in, prec_in, info, pobs, ky, ky_first, kx, table, pert, cell, flag, innov, prec, sems):
    members, variables, zy, tx = pert.shape
    pairs = [(pert_in, pert), (cell_in, cell), (flag_in, flag), (innov_in, innov), (prec_in, prec)]
    copies = [pltpu.make_async_copy(a, b, sems.at[i]) for i, (a, b) in enumerate(pairs)]
    for copy in copies:
        copy.start()
    matrices(ty, ky, ky_first, kx)
    for copy in copies:
        copy.wait()
    half = tx // 2
    for m in range(members):
        for v in range(variables):
            block = split_x(pert[m, v].astype(F32).T)
            at = (m * variables + v) * half
            table[at : at + half, :] = block.astype(BF16)
    for j in range(0, cell.shape[0], CHUNK):
        k = chunk_of(cell, j)
        x, level_row = rem(k, tx), rem(over(k, tx), zy)
        hot = onehot_rows(over(x, half) * zy + level_row, 2 * zy)
        found = jnp.dot(table[...], hot, preferred_element_type=F32)
        want = over(k, tx * zy) * half + rem(x, half)
        rows = variables * half
        mask = iota((rows, k.shape[1]), 0) == jnp.broadcast_to(want, (rows, k.shape[1]))
        for m in range(members):
            got = jnp.where(mask, found[m * rows : (m + 1) * rows], 0.0)
            store_chunk(pobs.at[m], j, jnp.sum(got, axis=0, keepdims=True))
    k = cell[...]
    _, short = chunks(tx, wide, kx.shape[1])
    x = rem(k, tx)
    level_row = rem(over(k, tx), zy) - lax.axis_index("mem") * wide
    code = (over(x, short) * wide + level_row) * short + rem(x, short)
    info[0] = jnp.where((level_row >= 0) & (level_row < wide), code, -short).astype(F32)
    info[1] = jnp.where(flag[...] == 1, -prec[...], prec[...])
    info[2] = innov[...]


def decode(code, short):
    code = code.astype(jnp.int32)
    shift = short.bit_length() - 1
    return lax.shift_right_arithmetic(code, shift), code & (short - 1)


def send_strips(first, second, at, field):
    right, left = field[field.shape[0] - HALO :], field[:HALO]
    even = pair_side(lax.axis_index("gx")) == 1
    first[at] = jnp.where(even, right, left)
    second[at] = jnp.where(even, left, right)


def start_kernel(blocks, parts, *refs):
    tiles, refs = refs[:blocks], refs[blocks:]
    before, after, ky_first, info, refs = refs[0], refs[1], refs[2], refs[3], refs[4:]
    pobs, (y1, state, first, second, pack) = refs[:parts], refs[parts:]
    rows = before.shape[0] // blocks
    for b in range(blocks):
        own = tiles[b][...]
        at = slice(b * rows, (b + 1) * rows)
        wide = jnp.concatenate([own, before[at], after[at]], axis=0).T
        out = exact_dot(wide, ky_first[...])
        state[b] = wide[:, : own.shape[0]]
        y1[b] = out
        send_strips(first, second, b, out)
    pack[0:3] = info[...]
    at = 3
    for part in pobs:
        pack[at : at + part.shape[0]] = part[...]
        at += part.shape[0]


def x_smooth(matrix, fields, firsts, seconds):
    wide = [jnp.concatenate([f, l, r], axis=0) for f, l, r in zip(fields, firsts, seconds)]
    out = exact_dot(matrix, jnp.concatenate(wide, axis=1))
    zy = fields[0].shape[1]
    return [out[:, i * zy : (i + 1) * zy] for i in range(len(fields))]


def gather_at(groups, wide, pack, seen):
    tables = to_table(groups, wide)
    members, short = len(tables), tables[0].shape[0]
    parts = [halves(t) for t in tables]
    stacked = jnp.concatenate([p[0] for p in parts] + [p[1] for p in parts], axis=0)
    rows = members * short
    for j in range(0, pack.shape[1], CHUNK):
        row, low = decode(chunk_of(pack.at[0], j), short)
        hot = onehot_rows(row, stacked.shape[1])
        found = jnp.dot(stacked, hot, preferred_element_type=F32)
        low = jnp.broadcast_to(low, (short, low.shape[1]))
        mask = iota(low.shape, 0) == low
        total = None
        for m in range(members):
            both = found[m * short : (m + 1) * short] + found[rows + m * short : rows + (m + 1) * short]
            term = jnp.where(mask, both, 0.0) * jnp.broadcast_to(chunk_of(pack.at[3 + m], j), both.shape)
            total = term if total is None else total + term
        store_chunk(seen, j, jnp.sum(total, axis=0, keepdims=True))


def first_seen_kernel(wide, y1, from_first, from_second, kx, pack, smoothed, seen):
    each = range(y1.shape[0])
    outs = x_smooth(kx[0], [y1[b] for b in each], [from_first[b] for b in each], [from_second[b] for b in each])
    for b in each:
        smoothed[b] = outs[b]
    gather_at(outs, wide, pack, seen)


def step_rows(sums):
    total = jnp.sum(sums, axis=0, keepdims=True)
    lane = iota(total.shape, 1)
    g = jnp.sum(jnp.where(lane == 0, total, 0.0), axis=1, keepdims=True)
    c = jnp.sum(jnp.where(lane == 1, total, 0.0), axis=1, keepdims=True)
    return g / (g + c)


def scatter_kernel(has_step, wide, *refs):
    packs, incs = refs[0:3], refs[3:6]
    refs = refs[6:]
    if has_step:
        steps, sums = refs[0:3], refs[3]
        refs = refs[4:]
        step = step_rows(sums[...])
    ky, y1, y2, first, second, weights, vals = refs
    blocks, tx, lanes = y1.shape
    members = packs[0].shape[0] - 3
    parts, short = chunks(tx, wide, lanes)
    tiles = []
    for t in range(3):
        pack = packs[t]
        inc = incs[t][...]
        if has_step:
            inc = inc - step * steps[t][...]
        misfit = inc - pack[2]
        prec = pack[1]
        weight = jnp.where(prec < 0, 1.0 / jnp.sqrt(1.0 + misfit * misfit), 1.0)
        pw = jnp.abs(prec) * weight
        q = pw * misfit
        if t == 0:
            weights[...] = pw
        for m in range(members):
            val = pack[3 + m] * q
            high = val.astype(BF16).astype(F32)
            vals[2 * m] = high
            vals[2 * m + 1] = val - high
        acc = None
        for j in range(0, pack.shape[1], CHUNK):
            row, low = decode(chunk_of(pack.at[0], j), short)
            hot = onehot_rows(row, parts * wide)
            low = jnp.broadcast_to(low, (short, low.shape[1]))
            mask = iota(low.shape, 0) == low
            rows = []
            for i in range(2 * members):
                value = jnp.broadcast_to(chunk_of(vals.at[i], j), low.shape)
                rows.append(jnp.where(mask, value, 0.0).astype(BF16))
            part = lax.dot_general(jnp.concatenate(rows, axis=0), hot, (((1,), (1,)), ((), ())), preferred_element_type=F32)
            acc = part if acc is None else acc + part
        tables = []
        for m in range(members):
            at = 2 * m * short
            tables.append(acc[at : at + short] + acc[at + short : at + 2 * short])
        tiles.append(jnp.concatenate(from_table(tables, wide, lanes), axis=0))
    out = exact_dot(jnp.concatenate(tiles, axis=1), ky[...])
    for b in range(blocks):
        for i, y in enumerate((y1, y2)):
            field = out[b * tx : (b + 1) * tx, i * lanes : (i + 1) * lanes]
            y[b] = field
            send_strips(first, second, (i, b), field)


def gather_kernel(has_step, wide, *refs):
    y1, y2, from_first, from_second, kx, pack, weights, control, smoothed = refs[:9]
    refs = refs[9:]
    each = range(y1.shape[0])
    if has_step:
        old_grad, old_smooth, sums, new_control, new_smoothed = refs[:5]
        refs = refs[5:]
        step = step_rows(sums[...])
    grad_out, smooth_out, seen, to_all = refs[:4]
    once = x_smooth(kx[0], [y1[b] for b in each], [from_first[0, b] for b in each], [from_second[0, b] for b in each])
    twice = x_smooth(kx[1], [y2[b] for b in each], [from_first[1, b] for b in each], [from_second[1, b] for b in each])
    squares = None
    outs = []
    for b in each:
        v, s = control[b], smoothed[b]
        if has_step:
            v = v - step * old_grad[b]
            s = s - step * old_smooth[b]
            new_control[b] = v
            new_smoothed[b] = s
        grad = v + once[b]
        smooth_grad = s + twice[b]
        grad_out[b] = grad
        smooth_out[b] = smooth_grad
        outs.append(smooth_grad)
        part = jnp.sum(grad * grad, axis=0, keepdims=True)
        squares = part if squares is None else squares + part
        if len(refs) > 4 and b == y1.shape[0] - 1:
            refs[4][0] = v
            refs[4][1] = grad
    gather_at(outs, wide, pack, seen)
    total = seen[...]
    c = jnp.sum(jnp.sum(weights[...] * total * total, axis=0, keepdims=True), axis=1, keepdims=True)
    g = jnp.sum(squares, axis=1, keepdims=True)
    lane = iota(to_all.shape, 1)
    to_all[...] = jnp.where(lane == 0, g, jnp.where(lane == 1, c, 0.0))


def widen_kernel(pert, out):
    members, variables, zy, _ = pert.shape
    wide = zy // 2
    other = 1 - lax.axis_index("mem")
    for m in range(members):
        for v in range(variables):
            out[m, v] = pert[m, v, pl.ds(other * wide, wide), :].astype(F32)


def analysis_of(perts, smoothed, background, analysis, wide):
    variables = background.shape[0]
    for v in range(variables):
        inc = background[v]
        for m, pert in enumerate(perts):
            inc = inc + pert(v) * smoothed[m * wide : (m + 1) * wide]
        analysis[v] = inc


def final_pair_kernel(sums, control, grad, back, smoothed, smooth_grad, pert, pert_other, background, control_out, analysis):
    members, _, zy, _ = pert.shape
    wide = zy // 2
    mem = lax.axis_index("mem")
    step = step_rows(sums[...])
    mine = (control[0] - step * grad[0]).T
    other = (back[0] - step * back[1]).T
    for m in range(members):
        control_out[m, pl.ds(mem * wide, wide), :] = mine[m * wide : (m + 1) * wide]
        control_out[m, pl.ds((1 - mem) * wide, wide), :] = other[m * wide : (m + 1) * wide]
    fields = jnp.concatenate([(smoothed[b] - step * smooth_grad[b]).T for b in range(smoothed.shape[0])], axis=0)
    perts = [lambda v, m=m: pert[m, v, pl.ds(mem * wide, wide), :].astype(F32) for m in range(members)]
    perts += [lambda v, m=m: pert_other[m, v] for m in range(members)]
    analysis_of(perts, fields, background, analysis, wide)


def final_any_kernel(sums, control, grad, smoothed, smooth_grad, pert, background, control_out, analysis):
    members, _, wide, _ = pert.shape
    step = step_rows(sums[...])
    lanes = control.shape[2]
    for b in range(control.shape[0]):
        control_out[b * lanes : (b + 1) * lanes] = (control[b] - step * grad[b]).T
    fields = jnp.concatenate([(smoothed[b] - step * smooth_grad[b]).T for b in range(smoothed.shape[0])], axis=0)
    analysis_of([lambda v, m=m: pert[m, v] for m in range(members)], fields, background, analysis, wide)


VMEM = pl.BlockSpec(memory_space=pltpu.VMEM)


HBM = pl.BlockSpec(memory_space=pltpu.HBM)


def call(kernel, ins, outs, scratch=(), us=3.0, space=VMEM):
    shapes = [jax.ShapeDtypeStruct(s, F32) for s in outs]
    return pl.pallas_call(
        kernel,
        out_shape=shapes,
        in_specs=[space] * len(ins),
        out_specs=[VMEM] * len(outs),
        scratch_shapes=list(scratch),
        compiler_params=pltpu.CompilerParams(vmem_limit_bytes=16 << 20),
        cost_estimate=pl.CostEstimate(flops=int(us * 1e9), bytes_accessed=1 << 20, transcendentals=0),
    )(*ins)


def first_partner(i, n):
    return i ^ 1 if i ^ 1 < n else i


def second_partner(i, n):
    return (((i + 1) ^ 1) - 1) % n


def swap_first(value, axis):
    n = lax.axis_size(axis)
    return lax.ppermute(value, axis, [(i, first_partner(i, n)) for i in range(n)])


def swap_second(value, axis):
    n, k = lax.axis_size(axis), lax.axis_size("gx")
    if axis == "gx":
        return lax.ppermute(value, axis, [(i, second_partner(i, n)) for i in range(n)])
    sends = []
    for i in range(n):
        to = ((i + 1) ^ 1) - 1
        for g in range(k):
            sends.append((i * k + g, to * k + g if 0 <= to < n else i * k + first_partner(g, k)))
    return lax.ppermute(value, (axis, "gx"), sends)


def swap_pairs(value, axis):
    return [swap_first(value, axis), swap_second(value, axis)]


def swap_each(first, second, axis):
    return swap_first(first, axis), swap_second(second, axis)


def swap_mem(value):
    return lax.ppermute(value, "mem", [(0, 1), (1, 0)])


def levels_out(value):
    n = lax.axis_size("mem")
    wide = value.shape[-2] // n
    cut = value.reshape(value.shape[:-2] + (n, wide) + value.shape[-1:])
    sent = jnp.moveaxis(cut, -3, 0)
    got = lax.all_to_all(sent, "mem", 0, 0, tiled=True)
    return got.reshape((n * value.shape[0],) + value.shape[1:-2] + (wide,) + value.shape[-1:])


def per_device(perturbations, control, background, obs_cell, huber_flag, innovation, precision):
    members, variables, nz, ty, tx = perturbations.shape
    zy, n_mem = nz * ty, lax.axis_size("mem")
    wide = zy // n_mem
    lanes = 128
    blocks = members * zy // lanes
    obs = obs_cell.shape
    axes = ("mem", "gy", "gx")
    n_all = math.prod(lax.axis_size(a) for a in axes)
    everyone = members * n_mem
    pert = perturbations.reshape(members, variables, zy, tx)
    own = control.reshape(members, zy, tx)
    field = (blocks, tx, lanes)
    strip = (blocks, HALO, lanes)
    pair = n_mem == 2 and members * wide == lanes

    if pair:
        theirs, mine = call(
            lambda c, a, b, t: halves_kernel(c, b, a, t),
            [own],
            [(lanes, tx)] * 2,
            [pltpu.SemaphoreType.DMA((members, 2))],
            us=1.0,
            space=HBM,
        )
        tiles = [mine, swap_mem(theirs)]
    else:
        spread = levels_out(own).reshape(blocks * lanes, tx)
        tiles = [spread[b * lanes : (b + 1) * lanes] for b in range(blocks)]
    info, pobs, ky, ky_first, kx = call(
        functools.partial(prep_kernel, ty, wide),
        [pert, obs_cell, huber_flag, innovation, precision],
        [(3,) + obs, (members,) + obs, (3 * lanes, 2 * lanes), (lanes + 2 * lanes * RADIUS // ty, lanes), (2, tx, tx + 2 * HALO)],
        [
            pltpu.VMEM((members * variables * tx // 2, 2 * zy), BF16),
            pltpu.VMEM(pert.shape, BF16),
            pltpu.VMEM(obs, jnp.int32),
            pltpu.VMEM(obs, jnp.int32),
            pltpu.VMEM(obs, F32),
            pltpu.VMEM(obs, F32),
            pltpu.SemaphoreType.DMA((5,)),
        ],
        us=4.0,
        space=HBM,
    )
    first, second = call(functools.partial(strips_kernel, ty), tiles, [(blocks * lanes * RADIUS // ty, tx)] * 2, us=0.5)
    before, after = swap_each(first, second, "gy")
    if pair:
        pobs_parts = [pobs, swap_mem(pobs)]
    else:
        pobs_parts = [lax.all_gather(pobs, "mem", axis=0, tiled=True)]
    y1, state, first, second, pack = call(
        functools.partial(start_kernel, blocks, len(pobs_parts)),
        tiles + [before, after, ky_first, info] + pobs_parts,
        [field, field, strip, strip, (3 + everyone,) + obs],
        us=1.0,
    )
    from_first, from_second = swap_each(first, second, "gx")
    packs = [pack] + swap_pairs(pack, "gy")
    smoothed, seen = call(functools.partial(first_seen_kernel, wide), [y1, from_first, from_second, kx, pack], [field, obs], us=1.5)
    incs = [seen] + swap_pairs(seen, "gy")
    steps, sums, grad, smooth_grad = None, None, None, None
    double = (2,) + strip
    for iteration in range(ITERS):
        later, last = iteration > 0, iteration + 1 == ITERS
        ins = packs + incs + (steps + [sums] if later else []) + [ky]
        y1, y2, first, second, weights = call(
            functools.partial(scatter_kernel, later, wide),
            ins,
            [field, field, double, double, obs],
            [pltpu.VMEM((2 * everyone,) + obs, F32)],
            us=3.0,
        )
        from_first, from_second = swap_each(first, second, "gx")
        ins = [y1, y2, from_first, from_second, kx, pack, weights, state, smoothed]
        outs = [field, field, obs, (n_all, 128)]
        if later:
            ins += [grad, smooth_grad, sums]
            outs = [field, field] + outs
        if last and pair:
            outs = outs + [(2, tx, lanes)]
        result = list(call(functools.partial(gather_kernel, later, wide), ins, outs, us=1.5))
        if later:
            state, smoothed = result[:2]
            result = result[2:]
        grad, smooth_grad, seen, to_all = result[:4]
        if not last:
            steps = [seen] + swap_pairs(seen, "gy")
        sums = lax.all_to_all(to_all, axes, 0, 0, tiled=True)
    back_ground = background.reshape(variables, wide, tx)
    if pair:
        (sent,) = call(widen_kernel, [pert], [(members, variables, wide, tx)], us=1.0)
        pert_other = swap_mem(sent)
        back = swap_mem(result[4])
        control_out, analysis = call(
            final_pair_kernel,
            [sums, state, grad, back, smoothed, smooth_grad, pert, pert_other, back_ground],
            [(members, zy, tx), (variables, wide, tx)],
            us=1.5,
        )
    else:
        spread, analysis = call(
            final_any_kernel,
            [sums, state, grad, smoothed, smooth_grad, levels_out(pert.astype(F32)), back_ground],
            [(blocks * lanes, tx), (variables, wide, tx)],
            us=1.5,
        )
        cut = lax.all_to_all(spread.reshape(n_mem, members, wide, tx), "mem", 0, 0, tiled=True)
        control_out = jnp.moveaxis(cut, 0, 1)
    return analysis.reshape(background.shape), control_out.reshape(control.shape)


def solution(mesh):
    in_specs = (
        P("mem", None, None, "gy", "gx"),
        P("mem", None, "gy", "gx"),
        P(None, "mem", "gy", "gx"),
        P("gy", "gx"),
        P("gy", "gx"),
        P("gy", "gx"),
        P("gy", "gx"),
    )
    out_specs = (P(None, "mem", "gy", "gx"), P("mem", None, "gy", "gx"))

    return jax.shard_map(per_device, mesh=mesh, in_specs=in_specs, out_specs=out_specs, check_vma=False)
```

```python
import functools
import math

import jax
import jax.numpy as jnp
from jax import lax
from jax.experimental import pallas as pl
from jax.experimental.pallas import tpu as pltpu
from jax.sharding import PartitionSpec as P


ITERS = 2
RADIUS = 4
RAW = [math.exp(-o * o / 8.0) for o in range(-RADIUS, RADIUS + 1)]
TAPS = [r / sum(RAW) for r in RAW]
HALO = 2 * RADIUS
F32 = jnp.float32
BF16 = jnp.bfloat16
EXACT = lax.Precision.HIGHEST
CHUNK = 4


def iota(shape, dim):
    return lax.broadcasted_iota(jnp.int32, shape, dim)


def over(k, n):
    return lax.shift_right_logical(k, n.bit_length() - 1) if n & (n - 1) == 0 else k // n


def rem(k, n):
    return k & (n - 1) if n & (n - 1) == 0 else k % n


def tap(d):
    d = jnp.abs(d)
    value = jnp.zeros(d.shape, F32)
    for o in range(RADIUS + 1):
        value = jnp.where(d == o, TAPS[RADIUS + o], value)
    return value


def exact_dot(a, b):
    return jnp.dot(a, b, precision=EXACT, preferred_element_type=F32)


def split_dot(a, b):
    rows = a[0].shape[0]
    first = jnp.dot(jnp.concatenate(a, axis=0), b[0], preferred_element_type=F32)
    second = jnp.dot(a[0], b[1], preferred_element_type=F32)
    return first[:rows] + (first[rows:] + second)


def halves(f32):
    high = f32.astype(BF16)
    low = (f32 - high.astype(F32)).astype(BF16)
    return high, low


def at_lane_block(shape, wide, s):
    return over(iota(shape, 1), wide) == s


def moved(piece, source, target, wide):
    if source == target:
        return piece
    return pltpu.roll(piece, (target - source) * wide % piece.shape[1], 1)


def chunks(tx, wide, lanes):
    parts = 2 * lanes // wide
    return parts, tx // parts


def to_table(groups, wide):
    tx, lanes = groups[0].shape
    parts, short = chunks(tx, wide, lanes)
    per = lanes // wide
    tables = []
    for group in groups:
        for m in range(per):
            blocks = []
            for p in range(parts // per):
                block = None
                for s in range(per):
                    at = (p * per + s) * short
                    piece = moved(group[at : at + short], m, s, wide)
                    block = piece if block is None else jnp.where(at_lane_block(piece.shape, wide, s), piece, block)
                blocks.append(block)
            tables.append(jnp.concatenate(blocks, axis=1))
    return tables


def from_table(tables, wide, lanes, parts):
    per = lanes // wide
    groups = []
    for first in range(0, len(tables), per):
        rows = []
        for x in range(parts):
            p, s = x // per, x % per
            block = None
            for m in range(per):
                piece = moved(tables[first + m][:, p * lanes : (p + 1) * lanes], s, m, wide)
                block = piece if block is None else jnp.where(at_lane_block(piece.shape, wide, m), piece, block)
            rows.append(block)
        groups.append(jnp.concatenate(rows, axis=0))
    return groups


def onehot_rows(index, rows):
    wide = jnp.broadcast_to(index, (rows, index.shape[1]))
    return jnp.where(iota(wide.shape, 0) == wide, 1.0, 0.0).astype(BF16)


def chunk_of(ref, j):
    return jnp.concatenate([ref[j + i : j + i + 1, :] for i in range(CHUNK)], axis=1)


def store_chunk(ref, j, row):
    wide = row.shape[1] // CHUNK
    for i in range(CHUNK):
        ref[j + i : j + i + 1, :] = row[:, i * wide : (i + 1) * wide]


def pair_side(index):
    return jnp.where(rem(index, 2) == 0, 1, -1)


def y_geometry(k, zy, ty):
    gy, ngy = lax.axis_index("gy"), lax.axis_size("gy")
    tile, at = over(k, zy), rem(k, zy)
    side = pair_side(gy)
    where = gy + jnp.where(tile == 0, 0, jnp.where(tile == 1, side, -side))
    return over(at, ty), where * ty + rem(at, ty), (where >= 0) & (where < ngy)


def band_y(shape, zy, ty):
    zs, ys, oks = y_geometry(iota(shape, 0), zy, ty)
    zt, yt, okt = y_geometry(iota(shape, 1), zy, ty)
    return jnp.where((zs == zt) & oks & okt, tap(ys - yt), 0.0)


def band_x(shape, tx):
    gx, ngx = lax.axis_index("gx"), lax.axis_size("gx")
    side = pair_side(gx)

    def place(k):
        tile, r = jnp.where(k < tx, 0, jnp.where(k < tx + HALO, 1, 2)), rem(k - tx, HALO)
        right = (tile == 1) == (side == 1)
        at = jnp.where(tile == 0, k, jnp.where(right, tx + r, r - HALO))
        full = gx * tx + at
        return at, (full >= 0) & (full < ngx * tx)

    xt, okt = place(iota(shape, 0))
    xs, oks = place(iota(shape, 1))
    return jnp.where(oks & okt, tap(xs - xt), 0.0)


def once_matrices(ty, ky_first, kx):
    zy, tx = ky_first.shape[2], kx.shape[1]
    shape = ky_first.shape[1:]
    k = iota(shape, 0)
    gy, ngy = lax.axis_index("gy"), lax.axis_size("gy")
    rows = zy * RADIUS // ty
    tile = jnp.where(k < zy, 0, jnp.where(k < zy + rows, 1, 2))
    at = k - jnp.where(tile == 0, 0, jnp.where(tile == 1, zy, zy + rows))
    side = jnp.where(tile == 1, pair_side(gy), -pair_side(gy))
    strip_row = (gy + side) * ty + rem(at, RADIUS) + jnp.where(side == 1, 0, ty - RADIUS)
    row = jnp.where(tile == 0, gy * ty + rem(at, ty), strip_row)
    level = jnp.where(tile == 0, over(at, ty), over(at, RADIUS))
    zt, yt, _ = y_geometry(iota(shape, 1), zy, ty)
    ky_first[0], ky_first[1] = halves(jnp.where((level == zt) & (row >= 0) & (row < ngy * ty), tap(row - yt), 0.0))
    kx[0], kx[1] = halves(band_x(kx.shape[1:], tx))


def twice_matrices(ty, ky, kx):
    wide, zy = ky.shape[1], ky.shape[2] // 2
    tx = kx.shape[1]
    once = band_y((wide, zy), zy, ty)
    ky[0, :, :zy], ky[1, :, :zy] = halves(once)
    ky[0, :, zy:], ky[1, :, zy:] = halves(exact_dot(band_y((wide, wide), zy, ty), once))
    long = kx.shape[2]
    kx[0], kx[1] = halves(exact_dot(band_x((tx, long), tx), band_x((long, long), tx)))


def y_strips(ty, value):
    lanes, tx = value.shape
    next_first = pair_side(lax.axis_index("gy")) == 1
    rows = lanes * RADIUS // ty
    value = value.reshape(lanes // (2 * ty), 2, ty, tx)
    even, odd = value[:, 0], value[:, 1]
    low = iota(even.shape, 1) < RADIUS
    last = jnp.where(low, pltpu.roll(even, RADIUS, 1), odd).reshape(rows, tx)
    initial = jnp.where(low, even, pltpu.roll(odd, RADIUS, 1)).reshape(rows, tx)
    return jnp.where(next_first, last, initial), jnp.where(next_first, initial, last)


def cut_kernel(control, theirs, mine, sems):
    members, zy, _ = control.shape
    wide = zy // 2
    mem = lax.axis_index("mem")
    copies = []
    for m in range(members):
        for i, (target, part) in enumerate(((theirs, 1 - mem), (mine, mem))):
            source = control.at[m, pl.ds(pl.multiple_of(part * wide, wide), wide), :]
            copies.append(pltpu.make_async_copy(source, target.at[pl.ds(m * wide, wide), :], sems.at[m, i]))
    for copy in copies:
        copy.start()
    for copy in copies:
        copy.wait()


def strips_kernel(ty, *refs):
    *blocks, first, second = refs
    rows = first.shape[0] // len(blocks)
    for b, block in enumerate(blocks):
        at = slice(b * rows, (b + 1) * rows)
        first[at], second[at] = y_strips(ty, block[...])


def pobs_kernel(wide, short, pert, cell, flag, innov, prec, info, pobs):
    members, variables, zy, tx = pert.shape
    table = jnp.concatenate([pert[m].reshape(variables * zy, tx).astype(F32).T for m in range(members)], axis=0).astype(BF16)
    for j in range(0, cell.shape[0], CHUNK):
        k = chunk_of(cell, j)
        hot = onehot_rows(over(k, tx), variables * zy)
        found = jnp.dot(table, hot, preferred_element_type=F32)
        x = jnp.broadcast_to(rem(k, tx), (tx, k.shape[1]))
        mask = iota(x.shape, 0) == x
        for m in range(members):
            got = jnp.where(mask, found[m * tx : (m + 1) * tx], 0.0)
            store_chunk(pobs.at[m], j, jnp.sum(got, axis=0, keepdims=True))
    k = cell[...]
    x = rem(k, tx)
    level_row = rem(over(k, tx), zy) - lax.axis_index("mem") * wide
    code = (over(x, short) * wide + level_row) * short + rem(x, short)
    info[0] = jnp.where((level_row >= 0) & (level_row < wide), code, -short).astype(F32)
    info[1] = jnp.where(flag[...] == 1, -prec[...], prec[...])
    info[2] = innov[...]


def pack_kernel(info, *refs):
    *pobs, pack = refs
    pack[0:3] = info[...]
    at = 3
    for part in pobs:
        pack[at : at + part.shape[0]] = part[...]
        at += part.shape[0]


def decode(code, short):
    code = code.astype(jnp.int32)
    shift = short.bit_length() - 1
    return lax.shift_right_arithmetic(code, shift), code & (short - 1)


def send_strips(first, second, at, left, right):
    even = pair_side(lax.axis_index("gx")) == 1
    first[at] = jnp.where(even, right, left)
    second[at] = jnp.where(even, left, right)


def start_kernel(blocks, *refs):
    tiles, (before, after, ky_first, y1, state, first, second) = refs[:blocks], refs[blocks:]
    rows = before.shape[0] // blocks
    for b in range(blocks):
        at = slice(b * rows, (b + 1) * rows)
        wide = jnp.concatenate([tiles[b][...], before[at], after[at]], axis=0).T
        out = split_dot(halves(wide), (ky_first[0], ky_first[1]))
        state[b] = wide[:, : tiles[b].shape[0]]
        y1[b] = out
        send_strips(first, second, b, out[:HALO], out[out.shape[0] - HALO :])


def x_smooth(matrix, fields, firsts, seconds):
    wide = [jnp.concatenate([f, l, r], axis=0) for f, l, r in zip(fields, firsts, seconds)]
    out = split_dot((matrix[0], matrix[1]), halves(jnp.concatenate(wide, axis=1)))
    zy = fields[0].shape[1]
    return [out[:, i * zy : (i + 1) * zy] for i in range(len(fields))]


def gather_at(groups, wide, pack, seen):
    tables = to_table(groups, wide)
    members, short = len(tables), tables[0].shape[0]
    parts = [halves(t) for t in tables]
    stacked = jnp.concatenate([p[0] for p in parts] + [p[1] for p in parts], axis=0)
    rows = members * short
    for j in range(0, pack.shape[1], CHUNK):
        row, low = decode(chunk_of(pack.at[0], j), short)
        hot = onehot_rows(row, stacked.shape[1])
        found = jnp.dot(stacked, hot, preferred_element_type=F32)
        low = jnp.broadcast_to(low, (short, low.shape[1]))
        mask = iota(low.shape, 0) == low
        total = None
        for m in range(members):
            both = found[m * short : (m + 1) * short] + found[rows + m * short : rows + (m + 1) * short]
            term = both * jnp.broadcast_to(chunk_of(pack.at[3 + m], j), both.shape)
            total = term if total is None else total + term
        store_chunk(seen, j, jnp.sum(jnp.where(mask, total, 0.0), axis=0, keepdims=True))


def first_seen_kernel(wide, y1, from_first, from_second, kx, pack, smoothed, seen):
    each = range(y1.shape[0])
    outs = x_smooth(kx, [y1[b] for b in each], [from_first[b] for b in each], [from_second[b] for b in each])
    for b in each:
        smoothed[b] = outs[b]
    gather_at(outs, wide, pack, seen)


def step_rows(sums):
    total = jnp.sum(sums, axis=0, keepdims=True)
    lane = iota(total.shape, 1)
    g = jnp.sum(jnp.where(lane == 0, total, 0.0), axis=1, keepdims=True)
    c = jnp.sum(jnp.where(lane == 1, total, 0.0), axis=1, keepdims=True)
    return g / (g + c)


def scatter_tables(codes, vals, t, members, short, rows, decode_at):
    acc = None
    for j in range(0, codes.shape[0], CHUNK):
        row, low = decode_at(chunk_of(codes, j))
        hot = onehot_rows(row, rows)
        low = jnp.broadcast_to(low, (short, low.shape[1]))
        mask = iota(low.shape, 0) == low
        parts = []
        for i in range(2 * members):
            value = jnp.broadcast_to(chunk_of(vals.at[t, i], j), low.shape)
            parts.append(jnp.where(mask, value, 0.0).astype(BF16))
        part = lax.dot_general(jnp.concatenate(parts, axis=0), hot, (((1,), (1,)), ((), ())), preferred_element_type=F32)
        acc = part if acc is None else acc + part
    return [acc[2 * m * short : (2 * m + 1) * short] + acc[(2 * m + 1) * short : (2 * m + 2) * short] for m in range(members)]


def edge_kernel(has_step, wide, tx, *refs):
    packs, incs = refs[0:3], refs[3:6]
    refs = refs[6:]
    if has_step:
        steps, sums = refs[0:3], refs[3]
        refs = refs[4:]
        step = step_rows(sums[...])
    ky, first, second, weights, vals = refs
    members = packs[0].shape[0] - 3
    lanes = ky.shape[2] // 2
    parts, short = chunks(tx, wide, lanes)

    def at_edge(code):
        row, low = decode(code, short)
        part, level_row = over(row, wide), rem(row, wide)
        left = (row >= 0) & (part == 0) & (low < HALO)
        right = (row >= 0) & (part == parts - 1) & (low >= short - HALO)
        return jnp.where(left, level_row, jnp.where(right, wide + level_row, -1)), rem(low, HALO)

    tiles = []
    for t in range(3):
        pack = packs[t]
        inc = incs[t][...]
        if has_step:
            inc = inc - step * steps[t][...]
        misfit = inc - pack[2]
        prec = pack[1]
        weight = jnp.where(prec < 0, 1.0 / jnp.sqrt(1.0 + misfit * misfit), 1.0)
        pw = jnp.abs(prec) * weight
        q = pw * misfit
        if t == 0:
            weights[...] = pw
        for m in range(members):
            val = pack[3 + m] * q
            high = val.astype(BF16).astype(F32)
            vals[t, 2 * m] = high
            vals[t, 2 * m + 1] = val - high
        tables = scatter_tables(pack.at[0], vals, t, members, HALO, lanes, at_edge)
        tiles.append(jnp.concatenate(from_table(tables, wide, lanes, 2), axis=0))
    out = split_dot(halves(jnp.concatenate(tiles, axis=1)), (ky[0], ky[1]))
    for b in range(first.shape[1]):
        for i in range(2):
            field = out[2 * b * HALO : 2 * (b + 1) * HALO, i * lanes : (i + 1) * lanes]
            send_strips(first, second, (i, b), field[:HALO], field[HALO:])


def scatter_kernel(wide, *refs):
    packs, (vals, ky, y1, y2) = refs[0:3], refs[3:]
    blocks, tx, lanes = y1.shape
    members = packs[0].shape[0] - 3
    parts, short = chunks(tx, wide, lanes)
    tiles = []
    for t in range(3):
        tables = scatter_tables(packs[t].at[0], vals, t, members, short, parts * wide, lambda code: decode(code, short))
        tiles.append(jnp.concatenate(from_table(tables, wide, lanes, parts), axis=0))
    out = split_dot(halves(jnp.concatenate(tiles, axis=1)), (ky[0], ky[1]))
    for b in range(blocks):
        y1[b] = out[b * tx : (b + 1) * tx, :lanes]
        y2[b] = out[b * tx : (b + 1) * tx, lanes:]


def gather_kernel(has_step, wide, *refs):
    y1, y2, from_first, from_second, kx, kxx, pack, weights, control, smoothed = refs[:10]
    refs = refs[10:]
    each = range(y1.shape[0])
    if has_step:
        old_grad, old_smooth, sums, new_control, new_smoothed = refs[:5]
        refs = refs[5:]
        step = step_rows(sums[...])
    grad_out, smooth_out, seen, to_all = refs[:4]
    once = x_smooth(kx, [y1[b] for b in each], [from_first[0, b] for b in each], [from_second[0, b] for b in each])
    twice = x_smooth(kxx, [y2[b] for b in each], [from_first[1, b] for b in each], [from_second[1, b] for b in each])
    squares = None
    outs = []
    for b in each:
        v, s = control[b], smoothed[b]
        if has_step:
            v = v - step * old_grad[b]
            s = s - step * old_smooth[b]
            new_control[b] = v
            new_smoothed[b] = s
        grad = v + once[b]
        smooth_grad = s + twice[b]
        grad_out[b] = grad
        smooth_out[b] = smooth_grad
        outs.append(smooth_grad)
        part = jnp.sum(grad * grad, axis=0, keepdims=True)
        squares = part if squares is None else squares + part
        if len(refs) > 4 and b == y1.shape[0] - 1:
            refs[4][0] = v
            refs[4][1] = grad
    gather_at(outs, wide, pack, seen)
    total = seen[...]
    c = jnp.sum(jnp.sum(weights[...] * total * total, axis=0, keepdims=True), axis=1, keepdims=True)
    g = jnp.sum(squares, axis=1, keepdims=True)
    lane = iota(to_all.shape, 1)
    to_all[...] = jnp.where(lane == 0, g, jnp.where(lane == 1, c, 0.0))


def widen_kernel(pert, out):
    members, variables, zy, _ = pert.shape
    wide = zy // 2
    other = 1 - lax.axis_index("mem")
    for m in range(members):
        for v in range(variables):
            out[m, v] = pert[m, v, pl.ds(other * wide, wide), :].astype(F32)


def analysis_of(perts, smoothed, background, analysis, wide):
    variables = background.shape[0]
    for v in range(variables):
        inc = background[v]
        for m, pert in enumerate(perts):
            inc = inc + pert(v) * smoothed[m * wide : (m + 1) * wide]
        analysis[v] = inc


def final_pair_kernel(sums, control, grad, back, smoothed, smooth_grad, pert, pert_other, background, control_out, analysis):
    members, _, zy, _ = pert.shape
    wide = zy // 2
    mem = lax.axis_index("mem")
    step = step_rows(sums[...])
    mine = (control[0] - step * grad[0]).T
    other = (back[0] - step * back[1]).T
    for m in range(members):
        control_out[m, pl.ds(mem * wide, wide), :] = mine[m * wide : (m + 1) * wide]
        control_out[m, pl.ds((1 - mem) * wide, wide), :] = other[m * wide : (m + 1) * wide]
    fields = jnp.concatenate([(smoothed[b] - step * smooth_grad[b]).T for b in range(smoothed.shape[0])], axis=0)
    perts = [lambda v, m=m: pert[m, v, pl.ds(mem * wide, wide), :].astype(F32) for m in range(members)]
    perts += [lambda v, m=m: pert_other[m, v] for m in range(members)]
    analysis_of(perts, fields, background, analysis, wide)


def final_any_kernel(sums, control, grad, smoothed, smooth_grad, pert, background, control_out, analysis):
    members, _, wide, _ = pert.shape
    step = step_rows(sums[...])
    lanes = control.shape[2]
    for b in range(control.shape[0]):
        control_out[b * lanes : (b + 1) * lanes] = (control[b] - step * grad[b]).T
    fields = jnp.concatenate([(smoothed[b] - step * smooth_grad[b]).T for b in range(smoothed.shape[0])], axis=0)
    analysis_of([lambda v, m=m: pert[m, v] for m in range(members)], fields, background, analysis, wide)


VMEM = pl.BlockSpec(memory_space=pltpu.VMEM)


HBM = pl.BlockSpec(memory_space=pltpu.HBM)


def call(kernel, ins, outs, scratch=(), us=3.0, space=VMEM, kind=F32):
    shapes = [jax.ShapeDtypeStruct(s, kind) for s in outs]
    return pl.pallas_call(
        kernel,
        out_shape=shapes,
        in_specs=[space] * len(ins),
        out_specs=[VMEM] * len(outs),
        scratch_shapes=list(scratch),
        compiler_params=pltpu.CompilerParams(vmem_limit_bytes=16 << 20),
        cost_estimate=pl.CostEstimate(flops=int(us * 1e9), bytes_accessed=1 << 20, transcendentals=0),
    )(*ins)


def swap_over(value, axis, to):
    n, k = lax.axis_size(axis), lax.axis_size("gx")
    if axis == "gx":
        return lax.ppermute(value, axis, [(i, to(i, n) % n) for i in range(n)])
    sends = []
    for i in range(n):
        for g in range(k):
            inside = 0 <= to(i, n) < n
            sends.append((i * k + g, to(i, n) * k + g if inside else i * k + (g ^ 1 if g ^ 1 < k else g)))
    return lax.ppermute(value, (axis, "gx"), sends)


def swap_first(value, axis):
    return swap_over(value, axis, lambda i, n: i ^ 1)


def swap_second(value, axis):
    return swap_over(value, axis, lambda i, n: ((i + 1) ^ 1) - 1)


def swap_pairs(value, axis):
    return [swap_first(value, axis), swap_second(value, axis)]


def swap_x(first, second):
    near = swap_first(first, "gx")
    far = swap_second(second, "gx")
    return near, far


def swap_mem(value):
    return lax.ppermute(value, "mem", [(0, 1), (1, 0)])


def levels_out(value):
    n = lax.axis_size("mem")
    wide = value.shape[-2] // n
    cut = value.reshape(value.shape[:-2] + (n, wide) + value.shape[-1:])
    sent = jnp.moveaxis(cut, -3, 0)
    got = lax.all_to_all(sent, "mem", 0, 0, tiled=True)
    return got.reshape((n * value.shape[0],) + value.shape[1:-2] + (wide,) + value.shape[-1:])


def per_device(perturbations, control, background, obs_cell, huber_flag, innovation, precision):
    members, variables, nz, ty, tx = perturbations.shape
    zy, n_mem = nz * ty, lax.axis_size("mem")
    wide = zy // n_mem
    lanes = 128
    blocks = members * zy // lanes
    obs = obs_cell.shape
    axes = ("mem", "gy", "gx")
    n_all = math.prod(lax.axis_size(a) for a in axes)
    everyone = members * n_mem
    pert = perturbations.reshape(members, variables, zy, tx)
    own = control.reshape(members, zy, tx)
    field = (blocks, tx, lanes)
    strip = (blocks, HALO, lanes)
    pair = n_mem == 2 and members * wide == lanes

    edge = (blocks * lanes * RADIUS // ty, tx)
    short = chunks(tx, wide, lanes)[1]
    long = tx + 2 * HALO
    if pair:
        theirs, mine = call(
            cut_kernel,
            [pltpu.with_memory_space_constraint(own, pltpu.HBM)],
            [(lanes, tx)] * 2,
            [pltpu.SemaphoreType.DMA((members, 2))],
            us=1.0,
            space=HBM,
        )
        tiles = [mine, swap_mem(theirs)]
    else:
        spread = levels_out(own).reshape(blocks * lanes, tx)
        tiles = [spread[b * lanes : (b + 1) * lanes] for b in range(blocks)]
    info, pobs = call(
        functools.partial(pobs_kernel, wide, short),
        [pert, obs_cell, huber_flag, innovation, precision],
        [(3,) + obs, (members,) + obs],
        us=2.0,
    )
    first, second = call(functools.partial(strips_kernel, ty), tiles, [edge, edge], us=0.2)
    before, after = swap_first(first, "gy"), swap_second(second, "gy")
    if pair:
        pobs_parts = [pobs, swap_mem(pobs)]
    else:
        pobs_parts = [lax.all_gather(pobs, "mem", axis=0, tiled=True)]
    ky_first, kx = call(
        functools.partial(once_matrices, ty), [], [(2, lanes + 2 * lanes * RADIUS // ty, lanes), (2, tx, long)], us=0.3, kind=BF16
    )
    y1, state, first, second = call(
        functools.partial(start_kernel, blocks), tiles + [before, after, ky_first], [field, field, strip, strip], us=1.0
    )
    from_first, from_second = swap_x(first, second)
    (pack,) = call(pack_kernel, [info] + pobs_parts, [(3 + everyone,) + obs], us=0.3)
    packs = [pack] + swap_pairs(pack, "gy")
    smoothed, seen = call(functools.partial(first_seen_kernel, wide), [y1, from_first, from_second, kx, pack], [field, obs], us=1.5)
    incs = [seen] + swap_pairs(seen, "gy")
    ky, kxx = call(functools.partial(twice_matrices, ty), [], [(2, 3 * lanes, 2 * lanes), (2, tx, long)], us=1.5, kind=BF16)
    steps, sums, grad, smooth_grad = None, None, None, None
    double = (2,) + strip
    for iteration in range(ITERS):
        later, last = iteration > 0, iteration + 1 == ITERS
        ins = packs + incs + (steps + [sums] if later else []) + [ky]
        first, second, weights, vals = call(
            functools.partial(edge_kernel, later, wide, tx), ins, [double, double, obs, (3, 2 * everyone) + obs], us=1.0
        )
        from_first, from_second = swap_x(first, second)
        y1, y2 = call(functools.partial(scatter_kernel, wide), packs + [vals, ky], [field, field], us=2.5)
        ins = [y1, y2, from_first, from_second, kx, kxx, pack, weights, state, smoothed]
        outs = [field, field, obs, (n_all, 128)]
        if later:
            ins += [grad, smooth_grad, sums]
            outs = [field, field] + outs
        if last and pair:
            outs = outs + [(2, tx, lanes)]
        result = list(call(functools.partial(gather_kernel, later, wide), ins, outs, us=1.5))
        if later:
            state, smoothed = result[:2]
            result = result[2:]
        grad, smooth_grad, seen, to_all = result[:4]
        if not last:
            steps = [seen] + swap_pairs(seen, "gy")
        sums = lax.all_to_all(to_all, axes, 0, 0, tiled=True)
    back_ground = background.reshape(variables, wide, tx)
    if pair:
        (sent,) = call(widen_kernel, [pert], [(members, variables, wide, tx)], us=1.0)
        pert_other = swap_mem(sent)
        back = swap_mem(result[4])
        control_out, analysis = call(
            final_pair_kernel,
            [sums, state, grad, back, smoothed, smooth_grad, pert, pert_other, back_ground],
            [(members, zy, tx), (variables, wide, tx)],
            us=1.5,
        )
    else:
        spread, analysis = call(
            final_any_kernel,
            [sums, state, grad, smoothed, smooth_grad, levels_out(pert.astype(F32)), back_ground],
            [(blocks * lanes, tx), (variables, wide, tx)],
            us=1.5,
        )
        cut = lax.all_to_all(spread.reshape(n_mem, members, wide, tx), "mem", 0, 0, tiled=True)
        control_out = jnp.moveaxis(cut, 0, 1)
    return analysis.reshape(background.shape), control_out.reshape(control.shape)


def solution(mesh):
    in_specs = (
        P("mem", None, None, "gy", "gx"),
        P("mem", None, "gy", "gx"),
        P(None, "mem", "gy", "gx"),
        P("gy", "gx"),
        P("gy", "gx"),
        P("gy", "gx"),
        P("gy", "gx"),
    )
    out_specs = (P(None, "mem", "gy", "gx"), P("mem", None, "gy", "gx"))

    return jax.shard_map(per_device, mesh=mesh, in_specs=in_specs, out_specs=out_specs, check_vma=False)
```

```python
import functools
import math

import jax
import jax.numpy as jnp
from jax import lax
from jax.experimental import pallas as pl
from jax.experimental.pallas import tpu as pltpu
from jax.sharding import PartitionSpec as P


ITERS = 2
RADIUS = 4
RAW = [math.exp(-o * o / 8.0) for o in range(-RADIUS, RADIUS + 1)]
TAPS = [r / sum(RAW) for r in RAW]
HALO = 2 * RADIUS
F32 = jnp.float32
BF16 = jnp.bfloat16
EXACT = lax.Precision.HIGHEST
CHUNK = 4


def iota(shape, dim):
    return lax.broadcasted_iota(jnp.int32, shape, dim)


def over(k, n):
    return lax.shift_right_logical(k, n.bit_length() - 1) if n & (n - 1) == 0 else k // n


def rem(k, n):
    return k & (n - 1) if n & (n - 1) == 0 else k % n


def tap(d):
    d = jnp.abs(d)
    value = jnp.zeros(d.shape, F32)
    for o in range(RADIUS + 1):
        value = jnp.where(d == o, TAPS[RADIUS + o], value)
    return value


def exact_dot(a, b):
    return jnp.dot(a, b, precision=EXACT, preferred_element_type=F32)


def split_dot(a, b):
    rows = a[0].shape[0]
    first = jnp.dot(jnp.concatenate(a, axis=0), b[0], preferred_element_type=F32)
    second = jnp.dot(a[0], b[1], preferred_element_type=F32)
    return first[:rows] + (first[rows:] + second)


def halves(f32):
    high = f32.astype(BF16)
    low = (f32 - high.astype(F32)).astype(BF16)
    return high, low


def at_lane_block(shape, wide, s):
    return over(iota(shape, 1), wide) == s


def moved(piece, source, target, wide):
    if source == target:
        return piece
    return pltpu.roll(piece, (target - source) * wide % piece.shape[1], 1)


def chunks(tx, wide, lanes):
    parts = 2 * lanes // wide
    return parts, tx // parts


def to_table(groups, wide):
    tx, lanes = groups[0].shape
    parts, short = chunks(tx, wide, lanes)
    per = lanes // wide
    tables = []
    for group in groups:
        for m in range(per):
            blocks = []
            for p in range(parts // per):
                block = None
                for s in range(per):
                    at = (p * per + s) * short
                    piece = moved(group[at : at + short], m, s, wide)
                    block = piece if block is None else jnp.where(at_lane_block(piece.shape, wide, s), piece, block)
                blocks.append(block)
            tables.append(jnp.concatenate(blocks, axis=1))
    return tables


def from_table(tables, wide, lanes, parts):
    per = lanes // wide
    groups = []
    for first in range(0, len(tables), per):
        rows = []
        for x in range(parts):
            p, s = x // per, x % per
            block = None
            for m in range(per):
                piece = moved(tables[first + m][:, p * lanes : (p + 1) * lanes], s, m, wide)
                block = piece if block is None else jnp.where(at_lane_block(piece.shape, wide, m), piece, block)
            rows.append(block)
        groups.append(jnp.concatenate(rows, axis=0))
    return groups


def onehot_rows(index, rows):
    wide = jnp.broadcast_to(index, (rows, index.shape[1]))
    return jnp.where(iota(wide.shape, 0) == wide, 1.0, 0.0).astype(BF16)


def chunk_of(ref, j):
    return jnp.concatenate([ref[j + i : j + i + 1, :] for i in range(CHUNK)], axis=1)


def store_chunk(ref, j, row):
    wide = row.shape[1] // CHUNK
    for i in range(CHUNK):
        ref[j + i : j + i + 1, :] = row[:, i * wide : (i + 1) * wide]


def pair_side(index):
    return jnp.where(rem(index, 2) == 0, 1, -1)


def y_geometry(k, zy, ty):
    gy, ngy = lax.axis_index("gy"), lax.axis_size("gy")
    tile, at = over(k, zy), rem(k, zy)
    side = pair_side(gy)
    where = gy + jnp.where(tile == 0, 0, jnp.where(tile == 1, side, -side))
    return over(at, ty), where * ty + rem(at, ty), (where >= 0) & (where < ngy)


def band_y(shape, zy, ty):
    zs, ys, oks = y_geometry(iota(shape, 0), zy, ty)
    zt, yt, okt = y_geometry(iota(shape, 1), zy, ty)
    return jnp.where((zs == zt) & oks & okt, tap(ys - yt), 0.0)


def band_x(shape, tx):
    gx, ngx = lax.axis_index("gx"), lax.axis_size("gx")
    side = pair_side(gx)

    def place(k):
        tile, r = jnp.where(k < tx, 0, jnp.where(k < tx + HALO, 1, 2)), rem(k - tx, HALO)
        right = (tile == 1) == (side == 1)
        at = jnp.where(tile == 0, k, jnp.where(right, tx + r, r - HALO))
        full = gx * tx + at
        return at, (full >= 0) & (full < ngx * tx)

    xt, okt = place(iota(shape, 0))
    xs, oks = place(iota(shape, 1))
    return jnp.where(oks & okt, tap(xs - xt), 0.0)


def once_matrices(ty, ky_first, kx):
    zy, tx = ky_first.shape[2], kx.shape[1]
    shape = ky_first.shape[1:]
    k = iota(shape, 0)
    gy, ngy = lax.axis_index("gy"), lax.axis_size("gy")
    rows = zy * RADIUS // ty
    tile = jnp.where(k < zy, 0, jnp.where(k < zy + rows, 1, 2))
    at = k - jnp.where(tile == 0, 0, jnp.where(tile == 1, zy, zy + rows))
    side = jnp.where(tile == 1, pair_side(gy), -pair_side(gy))
    strip_row = (gy + side) * ty + rem(at, RADIUS) + jnp.where(side == 1, 0, ty - RADIUS)
    row = jnp.where(tile == 0, gy * ty + rem(at, ty), strip_row)
    level = jnp.where(tile == 0, over(at, ty), over(at, RADIUS))
    zt, yt, _ = y_geometry(iota(shape, 1), zy, ty)
    ky_first[0], ky_first[1] = halves(jnp.where((level == zt) & (row >= 0) & (row < ngy * ty), tap(row - yt), 0.0))
    kx[0], kx[1] = halves(band_x(kx.shape[1:], tx))


def twice_matrices(ty, ky, kx):
    wide, zy = ky.shape[1], ky.shape[2] // 2
    tx = kx.shape[1]
    once = band_y((wide, zy), zy, ty)
    ky[0, :, :zy], ky[1, :, :zy] = halves(once)
    ky[0, :, zy:], ky[1, :, zy:] = halves(exact_dot(band_y((wide, wide), zy, ty), once))
    long = kx.shape[2]
    kx[0], kx[1] = halves(exact_dot(band_x((tx, long), tx), band_x((long, long), tx)))


def y_strips(ty, value):
    lanes, tx = value.shape
    next_first = pair_side(lax.axis_index("gy")) == 1
    rows = lanes * RADIUS // ty
    value = value.reshape(lanes // (2 * ty), 2, ty, tx)
    even, odd = value[:, 0], value[:, 1]
    low = iota(even.shape, 1) < RADIUS
    last = jnp.where(low, pltpu.roll(even, RADIUS, 1), odd).reshape(rows, tx)
    initial = jnp.where(low, even, pltpu.roll(odd, RADIUS, 1)).reshape(rows, tx)
    return jnp.where(next_first, last, initial), jnp.where(next_first, initial, last)


def cut_kernel(control, theirs, mine, sems):
    members, zy, _ = control.shape
    wide = zy // 2
    mem = lax.axis_index("mem")
    copies = []
    for m in range(members):
        for i, (target, part) in enumerate(((theirs, 1 - mem), (mine, mem))):
            source = control.at[m, pl.ds(pl.multiple_of(part * wide, wide), wide), :]
            copies.append(pltpu.make_async_copy(source, target.at[pl.ds(m * wide, wide), :], sems.at[m, i]))
    for copy in copies:
        copy.start()
    for copy in copies:
        copy.wait()


def strips_kernel(ty, *refs):
    *blocks, first, second = refs
    rows = first.shape[0] // len(blocks)
    for b, block in enumerate(blocks):
        at = slice(b * rows, (b + 1) * rows)
        first[at], second[at] = y_strips(ty, block[...])


def pobs_kernel(wide, short, pert, cell, flag, innov, prec, info, pobs):
    members, variables, zy, tx = pert.shape
    table = jnp.concatenate([pert[m].reshape(variables * zy, tx).astype(F32).T for m in range(members)], axis=0).astype(BF16)
    for j in range(0, cell.shape[0], CHUNK):
        k = chunk_of(cell, j)
        hot = onehot_rows(over(k, tx), variables * zy)
        found = jnp.dot(table, hot, preferred_element_type=F32)
        x = jnp.broadcast_to(rem(k, tx), (tx, k.shape[1]))
        mask = iota(x.shape, 0) == x
        for m in range(members):
            got = jnp.where(mask, found[m * tx : (m + 1) * tx], 0.0)
            store_chunk(pobs.at[m], j, jnp.sum(got, axis=0, keepdims=True))
    k = cell[...]
    x = rem(k, tx)
    level_row = rem(over(k, tx), zy) - lax.axis_index("mem") * wide
    code = (over(x, short) * wide + level_row) * short + rem(x, short)
    info[0] = jnp.where((level_row >= 0) & (level_row < wide), code, -short).astype(F32)
    info[1] = jnp.where(flag[...] == 1, -prec[...], prec[...])
    info[2] = innov[...]


def pack_kernel(info, *refs):
    *pobs, pack = refs
    pack[0:3] = info[...]
    at = 3
    for part in pobs:
        pack[at : at + part.shape[0]] = part[...]
        at += part.shape[0]


def decode(code, short):
    code = code.astype(jnp.int32)
    shift = short.bit_length() - 1
    return lax.shift_right_arithmetic(code, shift), code & (short - 1)


def send_strips(first, second, at, left, right):
    even = pair_side(lax.axis_index("gx")) == 1
    first[at] = jnp.where(even, right, left)
    second[at] = jnp.where(even, left, right)


def start_kernel(blocks, *refs):
    tiles, (before, after, ky_first, y1, state, first, second) = refs[:blocks], refs[blocks:]
    rows = before.shape[0] // blocks
    for b in range(blocks):
        at = slice(b * rows, (b + 1) * rows)
        wide = jnp.concatenate([tiles[b][...], before[at], after[at]], axis=0).T
        out = split_dot(halves(wide), (ky_first[0], ky_first[1]))
        state[b] = wide[:, : tiles[b].shape[0]]
        y1[b] = out
        send_strips(first, second, b, out[:HALO], out[out.shape[0] - HALO :])


def x_smooth(matrix, fields, firsts, seconds):
    wide = [jnp.concatenate([f, l, r], axis=0) for f, l, r in zip(fields, firsts, seconds)]
    out = split_dot((matrix[0], matrix[1]), halves(jnp.concatenate(wide, axis=1)))
    zy = fields[0].shape[1]
    return [out[:, i * zy : (i + 1) * zy] for i in range(len(fields))]


def gather_at(groups, wide, pack, seen, places):
    tables = to_table(groups, wide)
    members, short = len(tables), tables[0].shape[0]
    parts = [halves(t) for t in tables]
    stacked = jnp.concatenate([p[0] for p in parts] + [p[1] for p in parts], axis=0)
    rows = members * short
    places[0], places[1] = decode(pack[0], short)
    for j in range(0, pack.shape[1], CHUNK):
        hot = onehot_rows(chunk_of(places.at[0], j), stacked.shape[1])
        found = jnp.dot(stacked, hot, preferred_element_type=F32)
        low = chunk_of(places.at[1], j)
        low = jnp.broadcast_to(low, (short, low.shape[1]))
        mask = iota(low.shape, 0) == low
        total = None
        for m in range(members):
            both = found[m * short : (m + 1) * short] + found[rows + m * short : rows + (m + 1) * short]
            term = both * jnp.broadcast_to(chunk_of(pack.at[3 + m], j), both.shape)
            total = term if total is None else total + term
        store_chunk(seen, j, jnp.sum(jnp.where(mask, total, 0.0), axis=0, keepdims=True))


def first_seen_kernel(wide, y1, from_first, from_second, kx, pack, smoothed, seen, places):
    each = range(y1.shape[0])
    outs = x_smooth(kx, [y1[b] for b in each], [from_first[b] for b in each], [from_second[b] for b in each])
    for b in each:
        smoothed[b] = outs[b]
    gather_at(outs, wide, pack, seen, places)


def step_rows(sums):
    total = jnp.sum(sums, axis=0, keepdims=True)
    lane = iota(total.shape, 1)
    g = jnp.sum(jnp.where(lane == 0, total, 0.0), axis=1, keepdims=True)
    c = jnp.sum(jnp.where(lane == 1, total, 0.0), axis=1, keepdims=True)
    return g / (g + c)


def scatter_tables(places, vals, t, members, short, rows):
    acc = None
    for j in range(0, places.shape[1], CHUNK):
        hot = onehot_rows(chunk_of(places.at[0], j), rows)
        low = chunk_of(places.at[1], j)
        low = jnp.broadcast_to(low, (short, low.shape[1]))
        mask = iota(low.shape, 0) == low
        parts = []
        for i in range(2 * members):
            value = jnp.broadcast_to(chunk_of(vals.at[t, i], j), low.shape)
            parts.append(jnp.where(mask, value, 0.0).astype(BF16))
        part = lax.dot_general(jnp.concatenate(parts, axis=0), hot, (((1,), (1,)), ((), ())), preferred_element_type=F32)
        acc = part if acc is None else acc + part
    return [acc[2 * m * short : (2 * m + 1) * short] + acc[(2 * m + 1) * short : (2 * m + 2) * short] for m in range(members)]


def beside(tables, per):
    return [jnp.concatenate(tables[i : i + per], axis=1) for i in range(0, len(tables), per)]


def observation_terms(pack, inc, vals, t):
    misfit = inc - pack[2]
    prec = pack[1]
    weight = jnp.where(prec < 0, 1.0 / jnp.sqrt(1.0 + misfit * misfit), 1.0)
    pw = jnp.abs(prec) * weight
    q = pw * misfit
    for m in range(pack.shape[0] - 3):
        val = pack[3 + m] * q
        high = val.astype(BF16).astype(F32)
        vals[t, 2 * m] = high
        vals[t, 2 * m + 1] = val - high
    return pw


def edge_tile(pack, vals, t, wide, tx, lanes, places):
    members = pack.shape[0] - 3
    parts, short = chunks(tx, wide, lanes)
    row, low = decode(pack[0], short)
    part, level_row = over(row, wide), rem(row, wide)
    left = (row >= 0) & (part == 0) & (low < HALO)
    right = (row >= 0) & (part == parts - 1) & (low >= short - HALO)
    places[t, 0] = jnp.where(left | right, level_row, -1)
    places[t, 1] = jnp.where(right, HALO, 0) + rem(low, HALO)
    tables = scatter_tables(places.at[t], vals, t, members, 2 * HALO, wide)
    return jnp.concatenate(beside(tables, lanes // wide), axis=0)


def full_tile(pack, vals, t, wide, tx, lanes, places):
    members = pack.shape[0] - 3
    parts, short = chunks(tx, wide, lanes)
    places[t, 0], places[t, 1] = decode(pack[0], short)
    tables = scatter_tables(places.at[t], vals, t, members, short, parts * wide)
    return jnp.concatenate(from_table(tables, wide, lanes, parts), axis=0)


def own_kernel(wide, tx, lanes, pack, inc, weights, edge, full, vals, edge_places, places):
    weights[...] = observation_terms(pack, inc[...], vals, 0)
    edge[...] = edge_tile(pack, vals, 0, wide, tx, lanes, edge_places)
    full[...] = full_tile(pack, vals, 0, wide, tx, lanes, places)


def edge_kernel(has_step, wide, tx, *refs):
    count = 3 if has_step else 2
    packs, incs = refs[:count], refs[count : 2 * count]
    refs = refs[2 * count :]
    tiles = []
    if has_step:
        steps, sums = refs[0:3], refs[3]
        refs = refs[4:]
        step = step_rows(sums[...])
        ky, first, second, vals, weights, places = refs
    else:
        own, ky, first, second, vals, places = refs
        tiles.append(own[...])
    lanes = ky.shape[2] // 2
    for t in range(count):
        inc = incs[t][...]
        if has_step:
            inc = inc - step * steps[t][...]
        pw = observation_terms(packs[t], inc, vals, t)
        if has_step and t == 0:
            weights[...] = pw
        tiles.append(edge_tile(packs[t], vals, t, wide, tx, lanes, places))
    out = split_dot(halves(jnp.concatenate(tiles, axis=1)), (ky[0], ky[1]))
    for b in range(first.shape[1]):
        for i in range(2):
            field = out[2 * b * HALO : 2 * (b + 1) * HALO, i * lanes : (i + 1) * lanes]
            send_strips(first, second, (i, b), field[:HALO], field[HALO:])


def scatter_kernel(given, wide, *refs):
    count = 2 if given else 3
    packs, refs = refs[:count], refs[count:]
    tiles = []
    if given:
        tiles.append(refs[0][...])
        refs = refs[1:]
    vals, ky, y1, y2, places = refs
    blocks, tx, lanes = y1.shape
    for t in range(count):
        tiles.append(full_tile(packs[t], vals, t, wide, tx, lanes, places))
    out = split_dot(halves(jnp.concatenate(tiles, axis=1)), (ky[0], ky[1]))
    for b in range(blocks):
        y1[b] = out[b * tx : (b + 1) * tx, :lanes]
        y2[b] = out[b * tx : (b + 1) * tx, lanes:]


def gather_kernel(has_step, sent, wide, *refs):
    y1, y2, from_first, from_second, kx, kxx, pack, weights, control, smoothed = refs[:10]
    refs = refs[10:]
    each = range(y1.shape[0])
    if has_step:
        old_grad, old_smooth, sums, new_control, new_smoothed = refs[:5]
        refs = refs[5:]
        step = step_rows(sums[...])
    if sent:
        grad_out, smooth_out, row, back, seen, places = refs
    else:
        grad_out, smooth_out, row, seen, places = refs
    once = x_smooth(kx, [y1[b] for b in each], [from_first[0, b] for b in each], [from_second[0, b] for b in each])
    twice = x_smooth(kxx, [y2[b] for b in each], [from_first[1, b] for b in each], [from_second[1, b] for b in each])
    squares = None
    outs = []
    for b in each:
        v, s = control[b], smoothed[b]
        if has_step:
            v = v - step * old_grad[b]
            s = s - step * old_smooth[b]
            new_control[b] = v
            new_smoothed[b] = s
        grad = v + once[b]
        smooth_grad = s + twice[b]
        grad_out[b] = grad
        smooth_out[b] = smooth_grad
        outs.append(smooth_grad)
        part = jnp.sum(grad * grad, axis=0, keepdims=True)
        squares = part if squares is None else squares + part
        if sent and b == y1.shape[0] - 1:
            back[0] = v
            back[1] = grad
    gather_at(outs, wide, pack, seen, places)
    total = seen[...]
    c = jnp.sum(jnp.sum(weights[...] * total * total, axis=0, keepdims=True), axis=1, keepdims=True)
    g = jnp.sum(squares, axis=1, keepdims=True)
    lane = iota(row.shape, 1)
    row[...] = jnp.where(lane == 0, g, jnp.where(lane == 1, c, 0.0))


def widen_kernel(pert, out):
    members, variables, zy, _ = pert.shape
    wide = zy // 2
    other = 1 - lax.axis_index("mem")
    for m in range(members):
        for v in range(variables):
            out[m, v] = pert[m, v, pl.ds(other * wide, wide), :].astype(F32)


def analysis_of(perts, smoothed, background, analysis, wide):
    variables = background.shape[0]
    for v in range(variables):
        inc = background[v]
        for m, pert in enumerate(perts):
            inc = inc + pert(v) * smoothed[m * wide : (m + 1) * wide]
        analysis[v] = inc


def final_pair_kernel(sums, control, grad, back, smoothed, smooth_grad, pert, pert_other, background, control_out, analysis):
    members, _, zy, _ = pert.shape
    wide = zy // 2
    mem = lax.axis_index("mem")
    step = step_rows(sums[...])
    mine = (control[0] - step * grad[0]).T
    other = (back[0] - step * back[1]).T
    for m in range(members):
        control_out[m, pl.ds(mem * wide, wide), :] = mine[m * wide : (m + 1) * wide]
        control_out[m, pl.ds((1 - mem) * wide, wide), :] = other[m * wide : (m + 1) * wide]
    fields = jnp.concatenate([(smoothed[b] - step * smooth_grad[b]).T for b in range(smoothed.shape[0])], axis=0)
    perts = [lambda v, m=m: pert[m, v, pl.ds(mem * wide, wide), :].astype(F32) for m in range(members)]
    perts += [lambda v, m=m: pert_other[m, v] for m in range(members)]
    analysis_of(perts, fields, background, analysis, wide)


def final_any_kernel(sums, control, grad, smoothed, smooth_grad, pert, background, control_out, analysis):
    members, _, wide, _ = pert.shape
    step = step_rows(sums[...])
    lanes = control.shape[2]
    for b in range(control.shape[0]):
        control_out[b * lanes : (b + 1) * lanes] = (control[b] - step * grad[b]).T
    fields = jnp.concatenate([(smoothed[b] - step * smooth_grad[b]).T for b in range(smoothed.shape[0])], axis=0)
    analysis_of([lambda v, m=m: pert[m, v] for m in range(members)], fields, background, analysis, wide)


VMEM = pl.BlockSpec(memory_space=pltpu.VMEM)


HBM = pl.BlockSpec(memory_space=pltpu.HBM)


def call(kernel, ins, outs, scratch=(), us=3.0, space=VMEM, kind=F32):
    shapes = [jax.ShapeDtypeStruct(s, kind) for s in outs]
    return pl.pallas_call(
        kernel,
        out_shape=shapes,
        in_specs=[space] * len(ins),
        out_specs=[VMEM] * len(outs),
        scratch_shapes=list(scratch),
        compiler_params=pltpu.CompilerParams(vmem_limit_bytes=16 << 20),
        cost_estimate=pl.CostEstimate(flops=int(us * 1e9), bytes_accessed=1 << 20, transcendentals=0),
    )(*ins)


def swap_over(value, axis, to):
    n, k = lax.axis_size(axis), lax.axis_size("gx")
    if axis == "gx":
        return lax.ppermute(value, axis, [(i, to(i, n) % n) for i in range(n)])
    sends = []
    for i in range(n):
        for g in range(k):
            inside = 0 <= to(i, n) < n
            sends.append((i * k + g, to(i, n) * k + g if inside else i * k + (g ^ 1 if g ^ 1 < k else g)))
    return lax.ppermute(value, (axis, "gx"), sends)


def swap_first(value, axis):
    return swap_over(value, axis, lambda i, n: i ^ 1)


def swap_second(value, axis):
    return swap_over(value, axis, lambda i, n: ((i + 1) ^ 1) - 1)


def swap_pairs(value, axis):
    return [swap_first(value, axis), swap_second(value, axis)]


def swap_x(first, second):
    near = swap_first(first, "gx")
    far = swap_second(second, "gx")
    return near, far


def swap_mem(value):
    return lax.ppermute(value, "mem", [(0, 1), (1, 0)])


def levels_out(value):
    n = lax.axis_size("mem")
    wide = value.shape[-2] // n
    cut = value.reshape(value.shape[:-2] + (n, wide) + value.shape[-1:])
    sent = jnp.moveaxis(cut, -3, 0)
    got = lax.all_to_all(sent, "mem", 0, 0, tiled=True)
    return got.reshape((n * value.shape[0],) + value.shape[1:-2] + (wide,) + value.shape[-1:])


def per_device(perturbations, control, background, obs_cell, huber_flag, innovation, precision):
    members, variables, nz, ty, tx = perturbations.shape
    zy, n_mem = nz * ty, lax.axis_size("mem")
    wide = zy // n_mem
    lanes = 128
    blocks = members * zy // lanes
    obs = obs_cell.shape
    axes = ("mem", "gy", "gx")
    n_all = math.prod(lax.axis_size(a) for a in axes)
    everyone = members * n_mem
    pert = perturbations.reshape(members, variables, zy, tx)
    own = control.reshape(members, zy, tx)
    field = (blocks, tx, lanes)
    strip = (blocks, HALO, lanes)
    pair = n_mem == 2 and members * wide == lanes

    edge = (blocks * lanes * RADIUS // ty, tx)
    short = chunks(tx, wide, lanes)[1]
    long = tx + 2 * HALO
    if pair:
        theirs, mine = call(
            cut_kernel,
            [pltpu.with_memory_space_constraint(own, pltpu.HBM)],
            [(lanes, tx)] * 2,
            [pltpu.SemaphoreType.DMA((members, 2))],
            us=1.0,
            space=HBM,
        )
        tiles = [mine, swap_mem(theirs)]
    else:
        spread = levels_out(own).reshape(blocks * lanes, tx)
        tiles = [spread[b * lanes : (b + 1) * lanes] for b in range(blocks)]
    info, pobs = call(
        functools.partial(pobs_kernel, wide, short),
        [pert, obs_cell, huber_flag, innovation, precision],
        [(3,) + obs, (members,) + obs],
        us=2.0,
    )
    first, second = call(functools.partial(strips_kernel, ty), tiles, [edge, edge], us=0.2)
    before, after = swap_first(first, "gy"), swap_second(second, "gy")
    if pair:
        pobs_parts = [pobs, swap_mem(pobs)]
    else:
        pobs_parts = [lax.all_gather(pobs, "mem", axis=0, tiled=True)]
    ky_first, kx = call(
        functools.partial(once_matrices, ty), [], [(2, lanes + 2 * lanes * RADIUS // ty, lanes), (2, tx, long)], us=0.3, kind=BF16
    )
    y1, state, first, second = call(
        functools.partial(start_kernel, blocks), tiles + [before, after, ky_first], [field, field, strip, strip], us=1.0
    )
    from_first, from_second = swap_x(first, second)
    (pack,) = call(pack_kernel, [info] + pobs_parts, [(3 + everyone,) + obs], us=0.3)
    packs = [pack] + swap_pairs(pack, "gy")
    where = pltpu.VMEM((2,) + obs, jnp.int32)
    where_all = pltpu.VMEM((3, 2) + obs, jnp.int32)
    smoothed, seen = call(
        functools.partial(first_seen_kernel, wide), [y1, from_first, from_second, kx, pack], [field, obs], [where], us=1.5
    )
    incs = [seen] + swap_pairs(seen, "gy")
    ky, kxx = call(functools.partial(twice_matrices, ty), [], [(2, 3 * lanes, 2 * lanes), (2, tx, long)], us=1.5, kind=BF16)
    weights, own_edge, own_full = call(
        functools.partial(own_kernel, wide, tx, lanes),
        [pack, seen],
        [obs, (blocks * 2 * HALO, lanes), (blocks * tx, lanes)],
        [pltpu.VMEM((1, 2 * everyone) + obs, F32), where_all, where_all],
        us=1.5,
    )
    steps, sums, grad, smooth_grad = None, None, None, None
    double = (2,) + strip
    for iteration in range(ITERS):
        later, last = iteration > 0, iteration + 1 == ITERS
        count = 3 if later else 2
        known = [] if later else [own_edge]
        ins = packs[-count:] + incs[-count:] + (steps + [sums] if later else known) + [ky]
        outs = [double, double, (count, 2 * everyone) + obs] + ([obs] if later else [])
        first, second, vals, *own_weights = call(
            functools.partial(edge_kernel, later, wide, tx), ins, outs, [where_all], us=1.0
        )
        weights = own_weights[0] if later else weights
        from_first, from_second = swap_x(first, second)
        ins = packs[-count:] + ([] if later else [own_full]) + [vals, ky]
        y1, y2 = call(functools.partial(scatter_kernel, not later, wide), ins, [field, field], [where_all], us=2.5)
        ins = [y1, y2, from_first, from_second, kx, kxx, pack, weights, state, smoothed]
        outs = [field, field, (1, 128)]
        if later:
            ins += [grad, smooth_grad, sums]
            outs = [field, field] + outs
        sent = last and pair
        if sent:
            outs = outs + [(2, tx, lanes)]
        scratch = ([pltpu.VMEM(obs, F32)] if last else []) + [where]
        if not last:
            outs = outs + [obs]
        result = list(call(functools.partial(gather_kernel, later, sent, wide), ins, outs, scratch, us=1.5))
        if later:
            state, smoothed = result[:2]
            result = result[2:]
        grad, smooth_grad, row = result[:3]
        seen = result[-1]
        if not last:
            steps = [seen] + swap_pairs(seen, "gy")
        to_all = jnp.broadcast_to(row[None], (n_all, 1, 128))
        sums = lax.all_to_all(to_all, axes, 0, 0, tiled=True).reshape(n_all, 128)
    back_ground = background.reshape(variables, wide, tx)
    if pair:
        (sent,) = call(widen_kernel, [pert], [(members, variables, wide, tx)], us=1.0)
        pert_other = swap_mem(sent)
        back = swap_mem(result[3])
        control_out, analysis = call(
            final_pair_kernel,
            [sums, state, grad, back, smoothed, smooth_grad, pert, pert_other, back_ground],
            [(members, zy, tx), (variables, wide, tx)],
            us=1.5,
        )
    else:
        spread, analysis = call(
            final_any_kernel,
            [sums, state, grad, smoothed, smooth_grad, levels_out(pert.astype(F32)), back_ground],
            [(blocks * lanes, tx), (variables, wide, tx)],
            us=1.5,
        )
        cut = lax.all_to_all(spread.reshape(n_mem, members, wide, tx), "mem", 0, 0, tiled=True)
        control_out = jnp.moveaxis(cut, 0, 1)
    return analysis.reshape(background.shape), control_out.reshape(control.shape)


def solution(mesh):
    in_specs = (
        P("mem", None, None, "gy", "gx"),
        P("mem", None, "gy", "gx"),
        P(None, "mem", "gy", "gx"),
        P("gy", "gx"),
        P("gy", "gx"),
        P("gy", "gx"),
        P("gy", "gx"),
    )
    out_specs = (P(None, "mem", "gy", "gx"), P("mem", None, "gy", "gx"))

    return jax.shard_map(per_device, mesh=mesh, in_specs=in_specs, out_specs=out_specs, check_vma=False)
```
